512 devices in a mesh: rows: 32 (over y_lo, z, core), cols: 16 (over x, y_hi).
Axes of the slice: x: 4, y: 8 (y_hi: 4, y_lo: 2; y = y_hi * 2 + y_lo), z: 8, core: 2. Of those that a mesh axis runs over, the one named last changes fastest.
Arguments:
- pair_rep: bfloat16 [128, 4096, 128], P('rows', 'cols'), may hold values from -6 to 6
- project_weight: bfloat16 [128, 512], replicated, may hold values from -0.5 to 0.5
- output_weight: bfloat16 [128, 128], replicated, may hold values from -0.5 to 0.5
- pair_bias: bfloat16 [4, 4096, 4096], P(None, 'cols', 'rows'), may hold values from -4 to 300
- chain_valid: int32 [32], replicated, may hold values from 1 to 128, as said below
Outputs:
- update: bfloat16 [128, 4096, 128], P('rows', 'cols')
The draws below stay inside these ranges and needn't reach their ends.
Inputs may be any that keep to these rules, and one draw needn't show every extreme that they name: Chain c occupies residues c * 128 to (c + 1) * 128 - 1; its first chain_valid[c] residues are valid; some chain is full.
All inputs are finite; a program needn't handle non-finite values.
Results may differ from the reference program's by a relative error of at most 0.0075.
Values may be sent and summed in bfloat16 or wider, within the bound.
No kernel may reach another device: no remote copies, remote signals or barrier semaphores. Data moves between devices by JAX's collectives and lax.ppermute only.
A program may use at most 64 MiB of HBM per device.

```python
import jax
import jax.numpy as jnp
from jax import lax

C = 128
H = 4
HD = 32
SLOT = 128
N = 4096
R = 128
CHAINS = 32


def draw_pair_bias(key, part):
    keys = jax.random.split(key, 1)
    base = jax.random.truncated_normal(keys[0], -4.0, 4.0, (H, N, N), jnp.float32)
    return base.astype(jnp.bfloat16)


def draw_chain_valid(key, part):
    keys = jax.random.split(jax.random.fold_in(key, 7), 2)
    counts = jax.random.randint(keys[0], (CHAINS,), 1, SLOT + 1)
    full_chain = jax.random.randint(keys[1], (), 0, CHAINS)
    return jnp.where(jnp.arange(CHAINS) == full_chain, SLOT, counts).astype(jnp.int32)


def levels(rng, shape, cuts, smallest, top_value):
    gain = 1.0
    for axis_at, parts in cuts:
        draws = jax.random.uniform(jax.random.fold_in(jax.random.fold_in(rng, 6), axis_at), (parts,), jnp.float32, smallest / len(cuts), top_value / len(cuts))
        gain = gain * jnp.repeat(jnp.exp(draws), shape[axis_at] // parts).reshape((-1,) + (1,) * (len(shape) - 1 - axis_at))
    return gain


def centred(rng, dims, deviation, bound, cuts=(), kind=jnp.bfloat16):
    loudness = levels(rng, dims, cuts, -0.22, 0.18) if cuts else 1.0
    values = jax.random.normal(rng, dims, jnp.float32) * deviation * loudness
    return jnp.minimum(jnp.maximum(values, -bound), bound).astype(kind)


def setup_inputs(seed: int = 0) -> dict:
    key_of = jax.random.split(jax.random.key(seed), 6)
    return {
        "pair_rep": centred(key_of[0], (R, N, C), 1.0, 6.0, ((0, 32), (1, 16))),
        "project_weight": centred(key_of[1], (C, 4 * H * HD), C ** -0.5, 0.5),
        "output_weight": centred(key_of[2], (H * HD, C), (H * HD) ** -0.5, 0.5),
        "pair_bias": draw_pair_bias(jax.random.fold_in(key_of[5], 71), 0),
        "chain_valid": draw_chain_valid(jax.random.fold_in(key_of[5], 71), 0),
    }


def reference(pair_rep, project_weight, output_weight, pair_bias, chain_valid):
    inner = H * HD
    pair_f = pair_rep.astype(jnp.float32)
    center = lax.optimization_barrier(jnp.mean(pair_f, axis=-1, keepdims=True))
    spread = lax.optimization_barrier(jnp.mean(jnp.square(pair_f - center), axis=-1, keepdims=True))
    normed = ((pair_f - center) * lax.rsqrt(spread + 1e-05)).astype(jnp.bfloat16)
    project = jnp.dot(normed.reshape(R * N, C), project_weight, preferred_element_type=jnp.float32)
    queries = (project[:, :inner] * HD ** (-0.5)).astype(jnp.bfloat16).reshape(R, N, H, HD)
    key_part = project[:, inner:2 * inner].astype(jnp.bfloat16).reshape(R, N, H, HD)
    value_part = project[:, 2 * inner:3 * inner].astype(jnp.bfloat16).reshape(R, N, H, HD)
    gate = jax.nn.sigmoid(project[:, 3 * inner:]).reshape(R, N, inner)
    position = jnp.arange(N, dtype=jnp.int32)
    allowed = chain_valid[position // SLOT]
    mask_add = jnp.where(position % SLOT < allowed, 0.0, -1000000000.0).astype(jnp.float32)
    bias_f = pair_bias.astype(jnp.float32)

    def one_row(items):
        query_row, key_row, value_row = items
        scores = jnp.einsum('jhd,khd->hjk', query_row.astype(jnp.float32), key_row.astype(jnp.float32))
        scores = scores + bias_f + mask_add[None, None, :]
        top = lax.optimization_barrier(jnp.max(scores, axis=-1, keepdims=True))
        expo = jnp.exp(scores - top)
        denom = lax.optimization_barrier(jnp.sum(expo, axis=-1))
        rounded = lax.optimization_barrier(expo.astype(jnp.bfloat16)).astype(jnp.float32)
        attended = jnp.einsum('hjk,khd->jhd', rounded, value_row.astype(jnp.float32))
        return attended / jnp.transpose(denom)[:, :, None]
    attended = lax.map(one_row, (queries, key_part, value_part))
    gated = (attended.reshape(R, N, inner) * gate).astype(jnp.bfloat16)
    update = jnp.dot(gated.reshape(R * N, inner), output_weight, preferred_element_type=jnp.float32)
    return update.astype(jnp.bfloat16).reshape(R, N, C)
```

```python
import functools

import jax
import jax.numpy as jnp
from jax import lax
from jax.experimental import pallas as pl
from jax.experimental.pallas import tpu as pltpu
from jax.sharding import PartitionSpec as P

SLOT = 128
GROUP = 16
BLOCK = 256
MASKED = -1000000000.0
LOG2E = 1.4426950408889634
REACH = 60.0
PAIR = 4

NT = (((1,), (1,)), ((), ()))
TN = (((0,), (0,)), ((), ()))


def prep_kernel(valid_ref, pair_ref, bias_ref, normed_ref, biast_ref):
    pair = pair_ref[...].astype(jnp.float32)
    center = jnp.mean(pair, axis=-1, keepdims=True)
    spread = jnp.mean(jnp.square(pair - center), axis=-1, keepdims=True)
    normed_ref[...] = ((pair - center) * lax.rsqrt(spread + 1e-05)).astype(jnp.bfloat16)
    heads, queries, keys = bias_ref.shape
    live = lax.broadcasted_iota(jnp.int32, (keys, queries), 0) < valid_ref[0]
    for head in range(heads):
        turned = jnp.transpose(bias_ref[head].astype(jnp.float32))
        biast_ref[head] = jnp.where(live, turned, MASKED).astype(jnp.bfloat16)


def prep(pair_rep, pair_bias, valid_here):
    heads, queries, keys = pair_bias.shape
    return pl.pallas_call(
        prep_kernel,
        out_shape=(
            jax.ShapeDtypeStruct(pair_rep.shape, jnp.bfloat16),
            jax.ShapeDtypeStruct((heads, keys, queries), jnp.bfloat16),
        ),
        in_specs=[
            pl.BlockSpec(memory_space=pltpu.SMEM),
            pl.BlockSpec(memory_space=pltpu.VMEM),
            pl.BlockSpec(memory_space=pltpu.VMEM),
        ],
        out_specs=(
            pl.BlockSpec(memory_space=pltpu.VMEM),
            pl.BlockSpec(memory_space=pltpu.VMEM),
        ),
        name="prep",
    )(valid_here, pair_rep, pair_bias)


def attend_kernel(
    groups_ref,
    start_ref,
    blocks_ref,
    order_ref,
    own_ref,
    near_ref,
    left_ref,
    right_ref,
    far_low_ref,
    far_high_ref,
    bias_ref,
    weight_ref,
    weight_t_ref,
    out_weight_ref,
    out_ref,
    packed,
    keys,
    values,
    queries,
    gates,
    gated,
    bias,
    shifted,
    sums,
    safe,
):
    rows, width = own_ref.shape[0], own_ref.shape[2]
    cols = own_ref.shape[1]
    chains = bias_ref.shape[0]
    inner = out_weight_ref.shape[0]
    heads = pl.num_programs(0)
    head = pl.program_id(0)
    head_size = inner // 4
    blocks = blocks_ref[0]
    total = blocks_ref[1]

    @pl.when(head == 0)
    def _():
        filler = jnp.zeros((GROUP, width), jnp.bfloat16)
        for row in range(rows):
            for group in range(BLOCK // GROUP):
                packed[row, pl.ds(pl.multiple_of(total + group * GROUP, GROUP), GROUP), :] = filler
        place = 0
        for pieces in (near_ref, left_ref, right_ref, far_low_ref, far_high_ref):
            for piece in range(pieces.shape[0]):
                for part in range(cols // SLOT):
                    chain = order_ref[place] * (cols // SLOT) + part
                    start = start_ref[chain]

                    def move(group, carry, pieces=pieces, piece=piece, part=part, start=start):
                        source = pl.multiple_of(part * SLOT + group * GROUP, GROUP)
                        target = pl.multiple_of(start + group * GROUP, GROUP)
                        for row in range(rows):
                            packed[row, pl.ds(target, GROUP), :] = pieces[
                                piece, row, pl.ds(source, GROUP), :
                            ]
                        return carry

                    lax.fori_loop(0, groups_ref[chain], move, 0)
                place += 1

        def project(block, peaks):
            fresh = []
            place = pl.ds(pl.multiple_of(block * BLOCK, BLOCK), BLOCK)
            for row in range(rows):
                part = packed[row, place, :]
                key_part = jnp.dot(
                    part, weight_ref[:, inner : 2 * inner], preferred_element_type=jnp.float32
                )
                keys[row, place, :] = key_part.astype(jnp.bfloat16)
                peak = jnp.max(jnp.abs(key_part).reshape(BLOCK // 8, 8, inner), axis=0)
                fresh.append(jnp.maximum(peaks[row], peak))
                turned = lax.dot_general(
                    weight_t_ref[2 * inner : 3 * inner, :],
                    part,
                    NT,
                    preferred_element_type=jnp.float32,
                ).astype(jnp.bfloat16)
                for h in range(4):
                    values[row, h, 0:head_size, place] = turned[h * head_size : (h + 1) * head_size]
                    values[row, h, head_size:, place] = jnp.ones(
                        (values.shape[2] - head_size, BLOCK), jnp.bfloat16
                    )
            return tuple(fresh)

        peaks = lax.fori_loop(
            0, blocks, project, tuple(jnp.zeros((8, inner), jnp.float32) for _ in range(rows))
        )
        reach = jnp.zeros((1, cols), jnp.float32)
        queries[...] = jnp.zeros_like(queries)
        for row in range(rows):
            own = own_ref[row]
            turned = lax.dot_general(
                weight_t_ref[0:inner, :], own, NT, preferred_element_type=jnp.float32
            )
            turned = (turned * head_size ** (-0.5)).astype(jnp.bfloat16)
            for h in range(4):
                span = slice(h * head_size, (h + 1) * head_size)
                queries[h, row, span, :] = turned[span]
            peak = jnp.max(peaks[row], axis=0, keepdims=True)
            peak = jnp.transpose(jnp.broadcast_to(peak, (inner, inner)))[:, 0:1]
            spread = jnp.abs(turned.astype(jnp.float32)) * peak
            for h in range(4):
                span = slice(h * head_size, (h + 1) * head_size)
                reach = jnp.maximum(reach, jnp.sum(spread[span], axis=0, keepdims=True))
            gate = jax.nn.sigmoid(
                lax.dot_general(
                    weight_t_ref[3 * inner : 4 * inner, :],
                    own,
                    NT,
                    preferred_element_type=jnp.float32,
                )
            )
            for h in range(4):
                gates[h, row] = gate[h * head_size : (h + 1) * head_size]
        safe[0] = (jnp.max(reach) < REACH).astype(jnp.int32)

    barrier = jnp.full((GROUP, cols), MASKED, jnp.bfloat16)
    for group in range(BLOCK // GROUP):
        bias[pl.ds(pl.multiple_of(total + group * GROUP, GROUP), GROUP), :] = barrier
    top = jnp.full((GROUP, cols), MASKED, jnp.bfloat16)
    for chain in range(chains):
        start = start_ref[chain]

        def move_bias(group, top, chain=chain, start=start):
            source = pl.multiple_of(group * GROUP, GROUP)
            target = pl.multiple_of(start + group * GROUP, GROUP)
            piece = bias_ref[chain, 0, pl.ds(source, GROUP), :]
            bias[pl.ds(target, GROUP), :] = piece
            return jnp.maximum(top, piece)

        top = lax.fori_loop(0, groups_ref[chain], move_bias, top)

    top = jnp.max(top.astype(jnp.float32), axis=0, keepdims=True)
    depth = values.shape[2]
    sums[...] = jnp.zeros_like(sums)

    @pl.when(safe[0] == 1)
    def _():
        def step(block, carry):
            place = pl.ds(pl.multiple_of(block * BLOCK, BLOCK), BLOCK)
            shifted[...] = (bias[place, :].astype(jnp.float32) - top) * LOG2E
            for pair in range(0, rows, PAIR):
                members = range(pair, pair + PAIR)
                scores = [
                    jnp.dot(
                        keys[row, place, :], queries[head, row], preferred_element_type=jnp.float32
                    )
                    for row in members
                ]
                weights = [
                    jnp.exp2(part * LOG2E + shifted[...]).astype(jnp.bfloat16) for part in scores
                ]
                for row, part in zip(members, weights):
                    sums[row] += jnp.dot(
                        values[row, head, :, place], part, preferred_element_type=jnp.float32
                    )
            return carry

        lax.fori_loop(0, blocks, step, 0)

    @pl.when(safe[0] == 0)
    def _():
        def step(block, state):
            place = pl.ds(pl.multiple_of(block * BLOCK, BLOCK), BLOCK)
            bias_block = bias[place, :].astype(jnp.float32)
            fresh = []
            for row in range(rows):
                scores = jnp.dot(
                    keys[row, place, :], queries[head, row], preferred_element_type=jnp.float32
                )
                scores = scores + bias_block
                new_max = jnp.maximum(state[row], jnp.max(scores, axis=0, keepdims=True))
                weights = jnp.exp(scores - new_max).astype(jnp.bfloat16)
                weighted = jnp.dot(
                    values[row, head, :, place], weights, preferred_element_type=jnp.float32
                )
                sums[row] = sums[row] * jnp.exp(state[row] - new_max) + weighted
                fresh.append(new_max)
            return tuple(fresh)

        lax.fori_loop(
            0,
            blocks,
            step,
            tuple(jnp.full((1, cols), -jnp.inf, jnp.float32) for _ in range(rows)),
        )

    for row in range(rows):
        total_row = sums[row]
        attended = total_row[0:head_size] / total_row[head_size : head_size + 1]
        gated[row, pl.ds(pl.multiple_of(head * head_size, head_size), head_size), :] = (
            attended * gates[head, row]
        ).astype(jnp.bfloat16)

    @pl.when(head == heads - 1)
    def _():
        for row in range(rows):
            out_ref[row] = lax.dot_general(
                gated[row], out_weight_ref[...], TN, preferred_element_type=jnp.float32
            ).astype(jnp.bfloat16)


def attend(normed, pieces, order, bias, project_weight, output_weight, chain_valid):
    rows, cols, width = normed.shape
    chains, heads, slot, _ = bias.shape
    inner = output_weight.shape[0]
    head_size = inner // heads
    groups = (chain_valid + GROUP - 1) // GROUP
    ends = jnp.cumsum(groups) * GROUP
    start = ends - groups * GROUP
    total = ends[-1]
    blocks = jnp.stack([(total + BLOCK - 1) // BLOCK, total])
    room = chains * slot + BLOCK
    depth = head_size + GROUP
    whole = lambda *shape: pl.BlockSpec(
        shape, lambda h, *_: (0,) * len(shape), pipeline_mode=pl.Buffered(1)
    )
    return pl.pallas_call(
        attend_kernel,
        grid_spec=pltpu.PrefetchScalarGridSpec(
            num_scalar_prefetch=4,
            grid=(heads,),
            in_specs=[
                whole(rows, cols, width),
                *(whole(*piece.shape) for piece in pieces),
                pl.BlockSpec((chains, 1, slot, cols), lambda h, *_: (0, h, 0, 0)),
                whole(width, 4 * inner),
                whole(4 * inner, width),
                whole(inner, output_weight.shape[1]),
            ],
            out_specs=pl.BlockSpec(
                (rows, cols, output_weight.shape[1]), lambda h, *_: (0, 0, 0)
            ),
            scratch_shapes=[
                pltpu.VMEM((rows, room, width), jnp.bfloat16),
                pltpu.VMEM((rows, room, inner), jnp.bfloat16),
                pltpu.VMEM((rows, heads, depth, room), jnp.bfloat16),
                pltpu.VMEM((heads, rows, inner, cols), jnp.bfloat16),
                pltpu.VMEM((heads, rows, head_size, cols), jnp.float32),
                pltpu.VMEM((rows, inner, cols), jnp.bfloat16),
                pltpu.VMEM((room, cols), jnp.bfloat16),
                pltpu.VMEM((BLOCK, cols), jnp.float32),
                pltpu.VMEM((rows, depth, cols), jnp.float32),
                pltpu.SMEM((1,), jnp.int32),
            ],
        ),
        out_shape=jax.ShapeDtypeStruct((rows, cols, output_weight.shape[1]), jnp.bfloat16),
        name="attend",
    )(
        groups,
        start,
        blocks,
        order,
        normed,
        *pieces,
        bias,
        project_weight,
        project_weight.T,
        output_weight,
    )


XS, YS = 4, 4


def shift(value, x_step, y_step):
    pairs = [
        (x * YS + y, (x + x_step) % XS * YS + (y + y_step) % YS)
        for x in range(XS)
        for y in range(YS)
    ]
    return lax.ppermute(value, "cols", pairs)


def gather_cols(own):
    above = shift(own, 0, 1)
    below = shift(own, 0, -1)
    across = shift(own, 0, 2)
    near = jnp.stack([own, above, below, across])
    left = shift(near, 1, 0)
    right = shift(near, -1, 0)
    far_low = shift(left[:2], 1, 0)
    far_high = shift(right[2:], -1, 0)
    here = lax.axis_index("cols")
    x, y = here // YS, here % YS
    y_of = jnp.stack([y, (y - 1) % YS, (y + 1) % YS, (y + 2) % YS])
    order = jnp.concatenate(
        [x * YS + y_of, (x - 1) % XS * YS + y_of, (x + 1) % XS * YS + y_of, (x + 2) % XS * YS + y_of]
    )
    return (near, left, right, far_low, far_high), order.astype(jnp.int32)


def local(pair_rep, project_weight, output_weight, pair_bias, chain_valid):
    here = lax.axis_index("rows")
    valid_here = lax.dynamic_slice_in_dim(chain_valid, here, 1, 0)
    normed, bias_t = prep(pair_rep, pair_bias, valid_here)
    bias = lax.all_gather(bias_t, "rows")
    pieces, order = gather_cols(normed)
    return attend(normed, pieces, order, bias, project_weight, output_weight, chain_valid)


def solution(mesh):
    return jax.shard_map(
        local,
        mesh=mesh,
        in_specs=(P("rows", "cols", None), P(), P(), P(None, "cols", "rows"), P()),
        out_specs=P("rows", "cols", None),
        check_vma=False,
    )
```

```python
import jax
import jax.numpy as jnp
from jax import lax
from jax.experimental import pallas as pl
from jax.experimental.pallas import tpu as pltpu
from jax.sharding import PartitionSpec as P


SLOT = 128
GROUP = 16
BLOCK = 256
MASKED = -1000000000.0
LOG2E = 1.4426950408889634
REACH = 60.0
PAIR = 4
XS, YS = 4, 4
PER_COL = 2
NEAR = 12 * PER_COL
FAR = 4 * PER_COL
NEAR_ROOM = NEAR * SLOT + BLOCK
FAR_ROOM = FAR * SLOT + BLOCK
ROOM = NEAR_ROOM + FAR_ROOM

NT = (((1,), (1,)), ((), ()))
TN = (((0,), (0,)), ((), ()))

SMEM = pl.BlockSpec(memory_space=pltpu.SMEM)
VMEM = pl.BlockSpec(memory_space=pltpu.VMEM)


def prep_kernel(valid_ref, pair_ref, bias_ref, normed_ref, biast_ref):
    pair = pair_ref[...].astype(jnp.float32)
    center = jnp.mean(pair, axis=-1, keepdims=True)
    spread = jnp.mean(jnp.square(pair - center), axis=-1, keepdims=True)
    normed_ref[...] = ((pair - center) * lax.rsqrt(spread + 1e-05)).astype(jnp.bfloat16)
    heads, queries, keys = bias_ref.shape
    valid = valid_ref[lax.axis_index("rows")]
    live = lax.broadcasted_iota(jnp.int32, (keys, queries), 0) < valid
    for head in range(heads):
        turned = jnp.transpose(bias_ref[head].astype(jnp.float32))
        biast_ref[head] = jnp.where(live, turned, MASKED).astype(jnp.bfloat16)


def prep(pair_rep, pair_bias, chain_valid):
    heads, queries, keys = pair_bias.shape
    return pl.pallas_call(
        prep_kernel,
        out_shape=(
            jax.ShapeDtypeStruct(pair_rep.shape, jnp.bfloat16),
            jax.ShapeDtypeStruct((heads, keys, queries), jnp.bfloat16),
        ),
        in_specs=[SMEM, VMEM, VMEM],
        out_specs=(VMEM, VMEM),
        name="prep",
    )(chain_valid, pair_rep, pair_bias)


def chart(valid_ref, table, places):
    col = lax.axis_index("cols")
    x, y = col >> 2, col & 3
    total = jnp.int32(0)
    for place in places:
        x_step = (0, 3, 1, 2)[place // (YS * PER_COL)]
        y_step = (0, 3, 1, 2)[place // PER_COL % YS]
        from_col = ((x + x_step) & (XS - 1)) * YS + ((y + y_step) & (YS - 1))
        chain = from_col * PER_COL + place % PER_COL
        table[0, place] = total
        table[1, place] = chain
        total = total + ((valid_ref[chain] + (GROUP - 1)) >> 4 << 4)
    table[2, places[0]] = total


def pack(table, places, refs, row, packed):
    sources = [
        (ref, piece, part)
        for ref in refs
        for piece in range(ref.shape[0])
        for part in range(PER_COL)
    ]
    total = table[2, places[0]]
    for (ref, piece, part), place in zip(sources, places):
        packed[pl.ds(pl.multiple_of(table[0, place], GROUP), SLOT), :] = ref[
            piece, row, part * SLOT : (part + 1) * SLOT, :
        ]
    packed[pl.ds(pl.multiple_of(total, GROUP), BLOCK), :] = jnp.zeros(
        (BLOCK, packed.shape[1]), jnp.bfloat16
    )


def project(packed, weight_ref, weight_t_ref, blocks, base, keys, values, peak):
    inner = weight_ref.shape[1] // 4
    heads, depth = values.shape[0], values.shape[1]
    head_size = inner // heads

    def step(block, peak):
        source = pl.ds(pl.multiple_of(block * BLOCK, BLOCK), BLOCK)
        place = pl.ds(pl.multiple_of(base + block * BLOCK, BLOCK), BLOCK)
        part = packed[source, :]
        key_part = jnp.dot(
            part, weight_ref[:, inner : 2 * inner], preferred_element_type=jnp.float32
        )
        turned = lax.dot_general(
            weight_t_ref[2 * inner : 3 * inner, :], part, NT, preferred_element_type=jnp.float32
        ).astype(jnp.bfloat16)
        keys[place, :] = key_part.astype(jnp.bfloat16)
        for h in range(heads):
            values[h, 0:head_size, place] = turned[h * head_size : (h + 1) * head_size]
            values[h, head_size:, place] = jnp.ones((depth - head_size, BLOCK), jnp.bfloat16)
        return jnp.maximum(
            peak, jnp.max(jnp.abs(key_part).reshape(BLOCK // 8, 8, inner), axis=0)
        )

    return lax.fori_loop(0, blocks, step, peak)


def near_kernel(
    valid_ref,
    own_ref,
    near_ref,
    left_ref,
    right_ref,
    weight_ref,
    weight_t_ref,
    keys_ref,
    values_ref,
    queries_ref,
    gates_ref,
    peaks_ref,
    packed,
    table,
):
    heads = queries_ref.shape[0]
    inner = queries_ref.shape[2]
    head_size = inner // heads
    own = own_ref[0]
    turned = lax.dot_general(weight_t_ref[0:inner, :], own, NT, preferred_element_type=jnp.float32)
    turned = (turned * head_size ** (-0.5)).astype(jnp.bfloat16)
    gate = jax.nn.sigmoid(
        lax.dot_general(
            weight_t_ref[3 * inner : 4 * inner, :], own, NT, preferred_element_type=jnp.float32
        )
    )
    queries_ref[...] = jnp.zeros_like(queries_ref)
    for h in range(heads):
        span = slice(h * head_size, (h + 1) * head_size)
        queries_ref[h, 0, span, :] = turned[span]
        gates_ref[h, 0] = gate[span]
    places = range(NEAR)

    @pl.when(pl.program_id(0) == 0)
    def _():
        chart(valid_ref, table, places)

    pack(table, places, (near_ref, left_ref, right_ref), 0, packed)
    blocks = (table[2, 0] + (BLOCK - 1)) >> 8
    peaks_ref[0] = project(
        packed,
        weight_ref,
        weight_t_ref,
        blocks,
        0,
        keys_ref.at[0],
        values_ref.at[0],
        jnp.zeros((8, inner), jnp.float32),
    )


def piece_spec(piece):
    count, _, cols, width = piece.shape
    return pl.BlockSpec((count, 1, cols, width), lambda i: (0, i, 0, 0))


def fixed(array):
    zeros = (0,) * array.ndim
    return pl.BlockSpec(array.shape, lambda i: zeros, pipeline_mode=pl.Buffered(1))


def project_near(chain_valid, normed, pieces, weight, weight_t, heads):
    rows, cols, width = normed.shape
    inner = weight.shape[1] // 4
    head_size = inner // heads
    depth = head_size + GROUP
    return pl.pallas_call(
        near_kernel,
        grid=(rows,),
        in_specs=[
            SMEM,
            pl.BlockSpec((1, cols, width), lambda i: (i, 0, 0)),
            *(piece_spec(piece) for piece in pieces),
            fixed(weight),
            fixed(weight_t),
        ],
        out_specs=(
            pl.BlockSpec((1, NEAR_ROOM, inner), lambda i: (i, 0, 0)),
            pl.BlockSpec((1, heads, depth, NEAR_ROOM), lambda i: (i, 0, 0, 0)),
            pl.BlockSpec((heads, 1, inner, cols), lambda i: (0, i, 0, 0)),
            pl.BlockSpec((heads, 1, head_size, cols), lambda i: (0, i, 0, 0)),
            pl.BlockSpec((1, 8, inner), lambda i: (i, 0, 0)),
        ),
        out_shape=(
            jax.ShapeDtypeStruct((rows, NEAR_ROOM, inner), jnp.bfloat16),
            jax.ShapeDtypeStruct((rows, heads, depth, NEAR_ROOM), jnp.bfloat16),
            jax.ShapeDtypeStruct((heads, rows, inner, cols), jnp.bfloat16),
            jax.ShapeDtypeStruct((heads, rows, head_size, cols), jnp.float32),
            jax.ShapeDtypeStruct((rows, 8, inner), jnp.float32),
        ),
        scratch_shapes=[
            pltpu.VMEM((NEAR * SLOT + BLOCK, width), jnp.bfloat16),
            pltpu.SMEM((3, NEAR + FAR), jnp.int32),
        ],
        name="near",
    )(chain_valid, normed, *pieces, weight, weight_t)


def attend_kernel(
    valid_ref,
    keys_hbm,
    values_hbm,
    low_ref,
    high_ref,
    weight_ref,
    weight_t_ref,
    queries,
    peaks_ref,
    gates,
    bias_ref,
    out_weight_ref,
    out_ref,
    keys,
    values,
    packed,
    gated,
    bias,
    shifted,
    sums,
    table,
    safe,
    sems,
):
    heads, rows, inner, cols = queries.shape
    head_size = inner // heads
    head = pl.program_id(0)
    half = bias_ref.shape[0]
    y_low = lax.axis_index("rows") >> 4
    spans = ((0, range(NEAR)), (NEAR_ROOM, range(NEAR, NEAR + FAR)))
    key_copy = pltpu.make_async_copy(keys_hbm, keys.at[:, pl.ds(0, NEAR_ROOM), :], sems.at[heads])

    def value_copy(h):
        return pltpu.make_async_copy(
            values_hbm.at[:, h], values.at[:, h, :, pl.ds(0, NEAR_ROOM)], sems.at[h]
        )

    @pl.when(head == 0)
    def _():
        key_copy.start()
        for h in range(heads):
            value_copy(h).start()
        for _, places in spans:
            chart(valid_ref, table, places)
        far = range(NEAR, NEAR + FAR)
        blocks = (table[2, NEAR] + (BLOCK - 1)) >> 8
        best = jnp.float32(0.0)
        for row in range(rows):
            pack(table, far, (low_ref, high_ref), row, packed)
            peak = project(
                packed,
                weight_ref,
                weight_t_ref,
                blocks,
                NEAR_ROOM,
                keys.at[row],
                values.at[row],
                peaks_ref[row],
            )
            peak = jnp.max(peak, axis=0, keepdims=True)
            peak = jnp.transpose(jnp.broadcast_to(peak, (inner, inner)))[:, 0:1]
            for h in range(heads):
                span = slice(h * head_size, (h + 1) * head_size)
                spread = jnp.abs(queries[h, row, span, :].astype(jnp.float32)) * peak[span]
                best = jnp.maximum(best, jnp.max(jnp.sum(spread, axis=0, keepdims=True)))
        safe[0] = (best < REACH).astype(jnp.int32)
        key_copy.wait()

    for h in range(heads):

        @pl.when(head == h)
        def _(h=h):
            value_copy(h).wait()

    top = jnp.full((GROUP, cols), MASKED, jnp.bfloat16)
    counts = []
    for base, places in spans:
        total = table[2, places[0]]

        def move(place, top, base=base):
            start, chain = table[0, place], table[1, place]
            piece = bias_ref[chain & (half - 1), (chain >> 4) ^ y_low, 0]
            bias[pl.ds(pl.multiple_of(base + start, GROUP), SLOT), :] = piece
            for group in range(0, SLOT, GROUP):
                top = jnp.maximum(top, piece[group : group + GROUP])
            return top

        top = lax.fori_loop(places[0], places[-1] + 1, move, top)
        bias[pl.ds(pl.multiple_of(base + total, GROUP), BLOCK), :] = jnp.full(
            (BLOCK, cols), MASKED, jnp.bfloat16
        )
        counts.append((total + (BLOCK - 1)) >> 8)
    near_blocks, blocks = counts[0], counts[0] + counts[1]
    top = jnp.max(top.astype(jnp.float32), axis=0, keepdims=True)
    sums[...] = jnp.zeros_like(sums)

    def place_of(block):
        block = jnp.where(block < near_blocks, block, block - near_blocks + NEAR_ROOM // BLOCK)
        return pl.ds(pl.multiple_of(block * BLOCK, BLOCK), BLOCK)

    @pl.when(safe[0] == 1)
    def _():
        def step(block, carry):
            place = place_of(block)
            shifted[...] = (bias[place, :].astype(jnp.float32) - top) * LOG2E
            for pair in range(0, rows, PAIR):
                members = range(pair, pair + PAIR)
                scores = [
                    jnp.dot(keys[row, place, :], queries[head, row], preferred_element_type=jnp.float32)
                    for row in members
                ]
                weights = [
                    jnp.exp2(part * LOG2E + shifted[...]).astype(jnp.bfloat16) for part in scores
                ]
                for row, part in zip(members, weights):
                    sums[row] += jnp.dot(
                        values[row, head, :, place], part, preferred_element_type=jnp.float32
                    )
            return carry

        lax.fori_loop(0, blocks, step, 0)

    @pl.when(safe[0] == 0)
    def _():
        def step(block, state):
            place = place_of(block)
            bias_block = bias[place, :].astype(jnp.float32)
            fresh = []
            for row in range(rows):
                scores = jnp.dot(
                    keys[row, place, :], queries[head, row], preferred_element_type=jnp.float32
                )
                scores = scores + bias_block
                new_max = jnp.maximum(state[row], jnp.max(scores, axis=0, keepdims=True))
                weights = jnp.exp(scores - new_max).astype(jnp.bfloat16)
                weighted = jnp.dot(
                    values[row, head, :, place], weights, preferred_element_type=jnp.float32
                )
                sums[row] = sums[row] * jnp.exp(state[row] - new_max) + weighted
                fresh.append(new_max)
            return tuple(fresh)

        lax.fori_loop(
            0,
            blocks,
            step,
            tuple(jnp.full((1, cols), -jnp.inf, jnp.float32) for _ in range(rows)),
        )

    for row in range(rows):
        total_row = sums[row]
        attended = total_row[0:head_size] / total_row[head_size : head_size + 1]
        gated[row, pl.ds(pl.multiple_of(head * head_size, head_size), head_size), :] = (
            attended * gates[0, row]
        ).astype(jnp.bfloat16)

    @pl.when(head == heads - 1)
    def _():
        for row in range(rows):
            out_ref[row] = lax.dot_general(
                gated[row], out_weight_ref[...], TN, preferred_element_type=jnp.float32
            ).astype(jnp.bfloat16)


def attend(
    chain_valid, keys, values, far, weight, weight_t, queries, peaks, gates, bias, output_weight
):
    heads, rows, inner, cols = queries.shape
    depth = values.shape[2]
    half, pair, _, slot, _ = bias.shape
    width = output_weight.shape[1]
    return pl.pallas_call(
        attend_kernel,
        grid=(heads,),
        in_specs=[
            SMEM,
            pl.BlockSpec(memory_space=pl.ANY),
            pl.BlockSpec(memory_space=pl.ANY),
            *(fixed(piece) for piece in far),
            fixed(weight),
            fixed(weight_t),
            fixed(queries),
            fixed(peaks),
            pl.BlockSpec((1, rows, inner // heads, cols), lambda h: (h, 0, 0, 0)),
            pl.BlockSpec((half, pair, 1, slot, cols), lambda h: (0, 0, h, 0, 0)),
            fixed(output_weight),
        ],
        out_specs=pl.BlockSpec((rows, cols, width), lambda h: (0, 0, 0)),
        scratch_shapes=[
            pltpu.VMEM((rows, ROOM, inner), jnp.bfloat16),
            pltpu.VMEM((rows, heads, depth, ROOM), jnp.bfloat16),
            pltpu.VMEM((FAR_ROOM, weight.shape[0]), jnp.bfloat16),
            pltpu.VMEM((rows, inner, cols), jnp.bfloat16),
            pltpu.VMEM((ROOM, cols), jnp.bfloat16),
            pltpu.VMEM((BLOCK, cols), jnp.float32),
            pltpu.VMEM((rows, depth, cols), jnp.float32),
            pltpu.SMEM((3, NEAR + FAR), jnp.int32),
            pltpu.SMEM((1,), jnp.int32),
            pltpu.SemaphoreType.DMA((heads + 1,)),
        ],
        out_shape=jax.ShapeDtypeStruct((rows, cols, width), jnp.bfloat16),
        name="attend",
    )(
        chain_valid,
        keys,
        values,
        *far,
        weight,
        weight_t,
        queries,
        peaks,
        gates,
        bias,
        output_weight,
    )


def shift(value, x_step, y_step):
    pairs = [
        (x * YS + y, (x + x_step) % XS * YS + (y + y_step) % YS)
        for x in range(XS)
        for y in range(YS)
    ]
    return lax.ppermute(value, "cols", pairs)


def gather_bias(bias_t):
    count = lax.axis_size("rows")
    half = count // 2
    swapped = lax.ppermute(bias_t, "rows", [(r, (r + half) % count) for r in range(count)])
    both = jnp.stack([bias_t, swapped])
    groups = [list(range(half)), list(range(half, count))]
    return lax.all_gather(both, "rows", axis_index_groups=groups)


def finish(chain_valid, normed, near, far, bias, project_weight, output_weight, heads):
    weight_t = project_weight.T
    keys, values, queries, gates, peaks = project_near(
        chain_valid, normed, near, project_weight, weight_t, heads
    )
    return attend(
        chain_valid,
        keys,
        values,
        far,
        project_weight,
        weight_t,
        queries,
        peaks,
        gates,
        bias,
        output_weight,
    )


def local(pair_rep, project_weight, output_weight, pair_bias, chain_valid):
    normed, bias_t = prep(pair_rep, pair_bias, chain_valid)
    bias = gather_bias(bias_t)
    above = shift(normed, 0, 1)
    below = shift(normed, 0, -1)
    across = shift(normed, 0, 2)
    near = jnp.stack([normed, above, below, across])
    left = shift(near, 1, 0)
    right = shift(near, -1, 0)
    far_low = shift(left[:2], 1, 0)
    far_high = shift(right[2:], -1, 0)
    return finish(
        chain_valid,
        normed,
        (near, left, right),
        (far_low, far_high),
        bias,
        project_weight,
        output_weight,
        pair_bias.shape[0],
    )


def solution(mesh):
    return jax.shard_map(
        local,
        mesh=mesh,
        in_specs=(P("rows", "cols", None), P(), P(), P(None, "cols", "rows"), P()),
        out_specs=P("rows", "cols", None),
        check_vma=False,
    )
```

```python
import jax
import jax.numpy as jnp
from jax import lax
from jax.experimental import pallas as pl
from jax.experimental.pallas import tpu as pltpu
from jax.sharding import PartitionSpec as P


SLOT = 128
GROUP = 16
BLOCK = 256
MASKED = -1000000000.0
LOG2E = 1.4426950408889634
REACH = 60.0
XS, YS = 4, 4
PER_COL = 2
NEAR = 12 * PER_COL
FAR = 4 * PER_COL
NEAR_ROOM = NEAR * SLOT + BLOCK
FAR_ROOM = FAR * SLOT + BLOCK
ROOM = NEAR_ROOM + FAR_ROOM

NT = (((1,), (1,)), ((), ()))
TN = (((0,), (0,)), ((), ()))

SMEM = pl.BlockSpec(memory_space=pltpu.SMEM)
VMEM = pl.BlockSpec(memory_space=pltpu.VMEM)


def prep_kernel(valid_ref, pair_ref, bias_ref, normed_ref, biast_ref):
    pair = pair_ref[...].astype(jnp.float32)
    center = jnp.mean(pair, axis=-1, keepdims=True)
    spread = jnp.mean(jnp.square(pair - center), axis=-1, keepdims=True)
    normed_ref[...] = ((pair - center) * lax.rsqrt(spread + 1e-05)).astype(jnp.bfloat16)
    heads, queries, keys = bias_ref.shape
    valid = valid_ref[lax.axis_index("rows")]
    live = lax.broadcasted_iota(jnp.int32, (keys, queries), 0) < valid
    for head in range(heads):
        turned = jnp.transpose(bias_ref[head].astype(jnp.float32))
        biast_ref[head] = jnp.where(live, turned, MASKED).astype(jnp.bfloat16)


def prep(pair_rep, pair_bias, chain_valid):
    heads, queries, keys = pair_bias.shape
    return pl.pallas_call(
        prep_kernel,
        out_shape=(
            jax.ShapeDtypeStruct(pair_rep.shape, jnp.bfloat16),
            jax.ShapeDtypeStruct((heads, keys, queries), jnp.bfloat16),
        ),
        in_specs=[SMEM, VMEM, VMEM],
        out_specs=(VMEM, VMEM),
        name="prep",
    )(chain_valid, pair_rep, pair_bias)


def chart(valid_ref, table, places):
    col = lax.axis_index("cols")
    x, y = col >> 2, col & 3
    total = jnp.int32(0)
    for place in places:
        x_step = (0, 3, 1, 2)[place // (YS * PER_COL)]
        y_step = (0, 3, 1, 2)[place // PER_COL % YS]
        from_col = ((x + x_step) & (XS - 1)) * YS + ((y + y_step) & (YS - 1))
        chain = from_col * PER_COL + place % PER_COL
        table[0, place] = total
        table[1, place] = chain
        total = total + ((valid_ref[chain] + (GROUP - 1)) >> 4 << 4)
    table[2, places[0]] = total


def pack(table, places, refs, row, packed):
    sources = [
        (ref, piece, part)
        for ref in refs
        for piece in range(ref.shape[0])
        for part in range(PER_COL)
    ]
    total = table[2, places[0]]
    for (ref, piece, part), place in zip(sources, places):
        packed[pl.ds(pl.multiple_of(table[0, place], GROUP), SLOT), :] = ref[
            piece, row, part * SLOT : (part + 1) * SLOT, :
        ]
    packed[pl.ds(pl.multiple_of(total, GROUP), BLOCK), :] = jnp.zeros(
        (BLOCK, packed.shape[1]), jnp.bfloat16
    )


def project(packed, weight_ref, weight_t_ref, blocks, base, keys, values, peak):
    inner = weight_ref.shape[1] // 4
    heads, depth = values.shape[0], values.shape[1]
    head_size = inner // heads

    def step(block, peak):
        source = pl.ds(pl.multiple_of(block * BLOCK, BLOCK), BLOCK)
        place = pl.ds(pl.multiple_of(base + block * BLOCK, BLOCK), BLOCK)
        part = packed[source, :]
        key_part = jnp.dot(
            part, weight_ref[:, inner : 2 * inner], preferred_element_type=jnp.float32
        )
        turned = lax.dot_general(
            weight_t_ref[2 * inner : 3 * inner, :], part, NT, preferred_element_type=jnp.float32
        ).astype(jnp.bfloat16)
        keys[place, :] = key_part.astype(jnp.bfloat16)
        for h in range(heads):
            values[h, 0:head_size, place] = turned[h * head_size : (h + 1) * head_size]
            values[h, head_size:, place] = jnp.ones((depth - head_size, BLOCK), jnp.bfloat16)
        return jnp.maximum(
            peak, jnp.max(jnp.abs(key_part).reshape(BLOCK // 8, 8, inner), axis=0)
        )

    return lax.fori_loop(0, blocks, step, peak)


def near_kernel(
    valid_ref,
    own_ref,
    others_ref,
    left_own_ref,
    left_ref,
    right_own_ref,
    right_ref,
    weight_ref,
    weight_t_ref,
    keys_ref,
    values_ref,
    queries_ref,
    gates_ref,
    peaks_ref,
    packed,
    table,
):
    heads = queries_ref.shape[0]
    inner = queries_ref.shape[2]
    head_size = inner // heads
    own = own_ref[0, 0]
    turned = lax.dot_general(weight_t_ref[0:inner, :], own, NT, preferred_element_type=jnp.float32)
    turned = (turned * head_size ** (-0.5)).astype(jnp.bfloat16)
    gate = jax.nn.sigmoid(
        lax.dot_general(
            weight_t_ref[3 * inner : 4 * inner, :], own, NT, preferred_element_type=jnp.float32
        )
    )
    queries_ref[...] = jnp.zeros_like(queries_ref)
    for h in range(heads):
        span = slice(h * head_size, (h + 1) * head_size)
        queries_ref[h, 0, span, :] = turned[span]
        gates_ref[h, 0] = gate[span]
    places = range(NEAR)

    @pl.when(pl.program_id(0) == 0)
    def _():
        chart(valid_ref, table, places)

    refs = (own_ref, others_ref, left_own_ref, left_ref, right_own_ref, right_ref)
    pack(table, places, refs, 0, packed)
    blocks = (table[2, 0] + (BLOCK - 1)) >> 8
    peaks_ref[0] = project(
        packed,
        weight_ref,
        weight_t_ref,
        blocks,
        0,
        keys_ref.at[0],
        values_ref.at[0],
        jnp.zeros((8, inner), jnp.float32),
    )


def piece_spec(piece):
    count, _, cols, width = piece.shape
    return pl.BlockSpec((count, 1, cols, width), lambda i: (0, i, 0, 0))


def fixed(array):
    zeros = (0,) * array.ndim
    return pl.BlockSpec(array.shape, lambda i: zeros, pipeline_mode=pl.Buffered(1))


def project_near(chain_valid, pieces, weight, weight_t, heads):
    _, rows, cols, width = pieces[0].shape
    inner = weight.shape[1] // 4
    head_size = inner // heads
    depth = head_size + GROUP
    return pl.pallas_call(
        near_kernel,
        grid=(rows,),
        in_specs=[
            SMEM,
            *(piece_spec(piece) for piece in pieces),
            fixed(weight),
            fixed(weight_t),
        ],
        out_specs=(
            pl.BlockSpec((1, NEAR_ROOM, inner), lambda i: (i, 0, 0)),
            pl.BlockSpec((1, heads, depth, NEAR_ROOM), lambda i: (i, 0, 0, 0)),
            pl.BlockSpec((heads, 1, inner, cols), lambda i: (0, i, 0, 0)),
            pl.BlockSpec((heads, 1, head_size, cols), lambda i: (0, i, 0, 0)),
            pl.BlockSpec((1, 8, inner), lambda i: (i, 0, 0)),
        ),
        out_shape=(
            jax.ShapeDtypeStruct((rows, NEAR_ROOM, inner), jnp.bfloat16),
            jax.ShapeDtypeStruct((rows, heads, depth, NEAR_ROOM), jnp.bfloat16),
            jax.ShapeDtypeStruct((heads, rows, inner, cols), jnp.bfloat16),
            jax.ShapeDtypeStruct((heads, rows, head_size, cols), jnp.float32),
            jax.ShapeDtypeStruct((rows, 8, inner), jnp.float32),
        ),
        scratch_shapes=[
            pltpu.VMEM((NEAR * SLOT + BLOCK, width), jnp.bfloat16),
            pltpu.SMEM((3, NEAR + FAR), jnp.int32),
        ],
        name="near",
    )(chain_valid, *pieces, weight, weight_t)


def attend_kernel(
    valid_ref,
    keys_hbm,
    values_hbm,
    low_ref,
    high_ref,
    weight_ref,
    weight_t_ref,
    queries,
    peaks_ref,
    gates,
    bias_ref,
    out_weight_ref,
    out_ref,
    keys,
    values,
    packed,
    gated,
    bias,
    shifted,
    sums,
    table,
    safe,
    sems,
):
    heads, rows, inner, cols = queries.shape
    head_size = inner // heads
    head = pl.program_id(0)
    half = bias_ref.shape[0]
    y_low = lax.axis_index("rows") >> 4
    spans = ((0, range(NEAR)), (NEAR_ROOM, range(NEAR, NEAR + FAR)))
    key_copy = pltpu.make_async_copy(keys_hbm, keys.at[:, pl.ds(0, NEAR_ROOM), :], sems.at[heads])

    def value_copy(h):
        return pltpu.make_async_copy(
            values_hbm.at[:, h], values.at[:, h, :, pl.ds(0, NEAR_ROOM)], sems.at[h]
        )

    @pl.when(head == 0)
    def _():
        key_copy.start()
        for h in range(heads):
            value_copy(h).start()
        for _, places in spans:
            chart(valid_ref, table, places)
        far = range(NEAR, NEAR + FAR)
        blocks = (table[2, NEAR] + (BLOCK - 1)) >> 8
        best = jnp.float32(0.0)
        for row in range(rows):
            pack(table, far, (low_ref, high_ref), row, packed)
            peak = project(
                packed,
                weight_ref,
                weight_t_ref,
                blocks,
                NEAR_ROOM,
                keys.at[row],
                values.at[row],
                peaks_ref[row],
            )
            peak = jnp.max(peak, axis=0, keepdims=True)
            peak = jnp.transpose(jnp.broadcast_to(peak, (inner, inner)))[:, 0:1]
            for h in range(heads):
                span = slice(h * head_size, (h + 1) * head_size)
                spread = jnp.abs(queries[h, row, span, :].astype(jnp.float32)) * peak[span]
                best = jnp.maximum(best, jnp.max(jnp.sum(spread, axis=0, keepdims=True)))
        safe[0] = (best < REACH).astype(jnp.int32)
        key_copy.wait()

    for h in range(heads):

        @pl.when(head == h)
        def _(h=h):
            value_copy(h).wait()

    top = jnp.full((GROUP, cols), MASKED, jnp.bfloat16)
    counts = []
    for base, places in spans:
        total = table[2, places[0]]

        def move(place, top, base=base):
            start, chain = table[0, place], table[1, place]
            piece = bias_ref[chain & (half - 1), (chain >> 4) ^ y_low, 0]
            bias[pl.ds(pl.multiple_of(base + start, GROUP), SLOT), :] = piece
            for group in range(0, SLOT, GROUP):
                top = jnp.maximum(top, piece[group : group + GROUP])
            return top

        top = lax.fori_loop(places[0], places[-1] + 1, move, top)
        bias[pl.ds(pl.multiple_of(base + total, GROUP), BLOCK), :] = jnp.full(
            (BLOCK, cols), MASKED, jnp.bfloat16
        )
        counts.append((total + (BLOCK - 1)) >> 8)
    near_blocks, blocks = counts[0], counts[0] + counts[1]
    top = jnp.max(top.astype(jnp.float32), axis=0, keepdims=True)
    sums[...] = jnp.zeros_like(sums)

    def place_of(block):
        block = jnp.where(block < near_blocks, block, block - near_blocks + NEAR_ROOM // BLOCK)
        return pl.ds(pl.multiple_of(block * BLOCK, BLOCK), BLOCK)

    @pl.when(safe[0] == 1)
    def _():
        def span(first, count):
            parts = [place_of(first + n) for n in range(count)]
            for n, place in enumerate(parts):
                shifted[n] = (bias[place, :].astype(jnp.float32) - top) * LOG2E
            weights = []
            for n, place in enumerate(parts):
                scores = [
                    jnp.dot(keys[row, place, :], queries[head, row], preferred_element_type=jnp.float32) for row in range(rows)
                ]
                weights.append(
                    [jnp.exp2(part * LOG2E + shifted[n]).astype(jnp.bfloat16) for part in scores]
                )
            for n, place in enumerate(parts):
                for row in range(rows):
                    sums[row] += jnp.dot(
                        values[row, head, :, place], weights[n][row], preferred_element_type=jnp.float32
                    )

        def double(pair, carry):
            span(2 * pair, 2)
            return carry

        lax.fori_loop(0, blocks >> 1, double, 0)

        @pl.when((blocks & 1) == 1)
        def _():
            span(blocks - 1, 1)

    @pl.when(safe[0] == 0)
    def _():
        def step(block, state):
            place = place_of(block)
            bias_block = bias[place, :].astype(jnp.float32)
            fresh = []
            for row in range(rows):
                scores = jnp.dot(
                    keys[row, place, :], queries[head, row], preferred_element_type=jnp.float32
                )
                scores = scores + bias_block
                new_max = jnp.maximum(state[row], jnp.max(scores, axis=0, keepdims=True))
                weights = jnp.exp(scores - new_max).astype(jnp.bfloat16)
                weighted = jnp.dot(
                    values[row, head, :, place], weights, preferred_element_type=jnp.float32
                )
                sums[row] = sums[row] * jnp.exp(state[row] - new_max) + weighted
                fresh.append(new_max)
            return tuple(fresh)

        lax.fori_loop(
            0,
            blocks,
            step,
            tuple(jnp.full((1, cols), -jnp.inf, jnp.float32) for _ in range(rows)),
        )

    for row in range(rows):
        total_row = sums[row]
        attended = total_row[0:head_size] / total_row[head_size : head_size + 1]
        gated[row, pl.ds(pl.multiple_of(head * head_size, head_size), head_size), :] = (
            attended * gates[0, row]
        ).astype(jnp.bfloat16)

    @pl.when(head == heads - 1)
    def _():
        for row in range(rows):
            out_ref[row] = lax.dot_general(
                gated[row], out_weight_ref[...], TN, preferred_element_type=jnp.float32
            ).astype(jnp.bfloat16)


def attend(
    chain_valid, keys, values, far, weight, weight_t, queries, peaks, gates, bias, output_weight
):
    heads, rows, inner, cols = queries.shape
    depth = values.shape[2]
    half, pair, _, slot, _ = bias.shape
    width = output_weight.shape[1]
    return pl.pallas_call(
        attend_kernel,
        grid=(heads,),
        in_specs=[
            SMEM,
            pl.BlockSpec(memory_space=pl.ANY),
            pl.BlockSpec(memory_space=pl.ANY),
            *(fixed(piece) for piece in far),
            fixed(weight),
            fixed(weight_t),
            fixed(queries),
            fixed(peaks),
            pl.BlockSpec((1, rows, inner // heads, cols), lambda h: (h, 0, 0, 0)),
            pl.BlockSpec((half, pair, 1, slot, cols), lambda h: (0, 0, h, 0, 0)),
            fixed(output_weight),
        ],
        out_specs=pl.BlockSpec((rows, cols, width), lambda h: (0, 0, 0)),
        scratch_shapes=[
            pltpu.VMEM((rows, ROOM, inner), jnp.bfloat16),
            pltpu.VMEM((rows, heads, depth, ROOM), jnp.bfloat16),
            pltpu.VMEM((FAR_ROOM, weight.shape[0]), jnp.bfloat16),
            pltpu.VMEM((rows, inner, cols), jnp.bfloat16),
            pltpu.VMEM((ROOM, cols), jnp.bfloat16),
            pltpu.VMEM((2, BLOCK, cols), jnp.float32),
            pltpu.VMEM((rows, depth, cols), jnp.float32),
            pltpu.SMEM((3, NEAR + FAR), jnp.int32),
            pltpu.SMEM((1,), jnp.int32),
            pltpu.SemaphoreType.DMA((heads + 1,)),
        ],
        out_shape=jax.ShapeDtypeStruct((rows, cols, width), jnp.bfloat16),
        name="attend",
    )(
        chain_valid,
        keys,
        values,
        *far,
        weight,
        weight_t,
        queries,
        peaks,
        gates,
        bias,
        output_weight,
    )


def shift(value, x_step, y_step):
    pairs = [
        (x * YS + y, (x + x_step) % XS * YS + (y + y_step) % YS)
        for x in range(XS)
        for y in range(YS)
    ]
    return lax.ppermute(value, "cols", pairs)


def gather_bias(bias_t):
    count = lax.axis_size("rows")
    half = count // 2
    swapped = lax.ppermute(bias_t, "rows", [(r, (r + half) % count) for r in range(count)])
    both = jnp.stack([bias_t, swapped])
    groups = [list(range(half)), list(range(half, count))]
    return lax.all_gather(both, "rows", axis_index_groups=groups)


def finish(chain_valid, near, far, bias, project_weight, output_weight, heads):
    weight_t = project_weight.T
    keys, values, queries, gates, peaks = project_near(
        chain_valid, near, project_weight, weight_t, heads
    )
    return attend(
        chain_valid,
        keys,
        values,
        far,
        project_weight,
        weight_t,
        queries,
        peaks,
        gates,
        bias,
        output_weight,
    )


def local(pair_rep, project_weight, output_weight, pair_bias, chain_valid):
    normed, bias_t = prep(pair_rep, pair_bias, chain_valid)
    bias = gather_bias(bias_t)
    left_own = shift(normed, 1, 0)
    right_own = shift(normed, -1, 0)
    above = shift(normed, 0, 1)
    below = shift(normed, 0, -1)
    across = shift(normed, 0, 2)
    others = jnp.stack([above, below, across])
    left = shift(others, 1, 0)
    right = shift(others, -1, 0)
    far_low = shift(jnp.stack([left_own, left[0]]), 1, 0)
    far_high = shift(right[1:], -1, 0)
    near = (normed[None], others, left_own[None], left, right_own[None], right)
    return finish(
        chain_valid,
        near,
        (far_low, far_high),
        bias,
        project_weight,
        output_weight,
        pair_bias.shape[0],
    )


def solution(mesh):
    return jax.shard_map(
        local,
        mesh=mesh,
        in_specs=(P("rows", "cols", None), P(), P(), P(None, "cols", "rows"), P()),
        out_specs=P("rows", "cols", None),
        check_vma=False,
    )
```

```python
import jax
import jax.numpy as jnp
from jax import lax
from jax.experimental import pallas as pl
from jax.experimental.pallas import tpu as pltpu
from jax.sharding import PartitionSpec as P


SLOT = 128
GROUP = 16
BLOCK = 256
MASKED = -1000000000.0
LOG2E = 1.4426950408889634
REACH = 60.0
XS, YS = 4, 4
PER_COL = 2
NEAR = 12 * PER_COL
FAR = 4 * PER_COL
NEAR_ROOM = NEAR * SLOT + BLOCK
FAR_ROOM = FAR * SLOT + BLOCK
ROOM = NEAR_ROOM + FAR_ROOM

NT = (((1,), (1,)), ((), ()))
TN = (((0,), (0,)), ((), ()))

SMEM = pl.BlockSpec(memory_space=pltpu.SMEM)
VMEM = pl.BlockSpec(memory_space=pltpu.VMEM)


def prep_kernel(valid_ref, pair_ref, bias_ref, normed_ref, biast_ref):
    pair = pair_ref[...].astype(jnp.float32)
    center = jnp.mean(pair, axis=-1, keepdims=True)
    spread = jnp.mean(jnp.square(pair - center), axis=-1, keepdims=True)
    normed_ref[...] = ((pair - center) * lax.rsqrt(spread + 1e-05)).astype(jnp.bfloat16)
    heads, queries, keys = bias_ref.shape
    valid = valid_ref[lax.axis_index("rows")]
    live = lax.broadcasted_iota(jnp.int32, (keys, queries), 0) < valid
    for head in range(heads):
        turned = jnp.transpose(bias_ref[head].astype(jnp.float32))
        biast_ref[head] = jnp.where(live, turned, MASKED).astype(jnp.bfloat16)


def prep(pair_rep, pair_bias, chain_valid):
    heads, queries, keys = pair_bias.shape
    return pl.pallas_call(
        prep_kernel,
        out_shape=(
            jax.ShapeDtypeStruct(pair_rep.shape, jnp.bfloat16),
            jax.ShapeDtypeStruct((heads, keys, queries), jnp.bfloat16),
        ),
        in_specs=[SMEM, VMEM, VMEM],
        out_specs=(VMEM, VMEM),
        name="prep",
    )(chain_valid, pair_rep, pair_bias)


def chart(valid_ref, table, places):
    col = lax.axis_index("cols")
    x, y = col >> 2, col & 3
    total = jnp.int32(0)
    for place in places:
        x_step = (0, 3, 1, 2)[place // (YS * PER_COL)]
        y_step = (0, 3, 1, 2)[place // PER_COL % YS]
        from_col = ((x + x_step) & (XS - 1)) * YS + ((y + y_step) & (YS - 1))
        chain = from_col * PER_COL + place % PER_COL
        table[0, place] = total
        table[1, place] = chain
        total = total + ((valid_ref[chain] + (GROUP - 1)) >> 4 << 4)
    table[2, places[0]] = total


def pack(table, places, refs, row, packed):
    sources = [
        (ref, piece, part)
        for ref in refs
        for piece in range(ref.shape[0])
        for part in range(PER_COL)
    ]
    total = table[2, places[0]]
    for (ref, piece, part), place in zip(sources, places):
        packed[pl.ds(pl.multiple_of(table[0, place], GROUP), SLOT), :] = ref[
            piece, row, part * SLOT : (part + 1) * SLOT, :
        ]
    packed[pl.ds(pl.multiple_of(total, GROUP), BLOCK), :] = jnp.zeros(
        (BLOCK, packed.shape[1]), jnp.bfloat16
    )


def project(packed, weight_ref, weight_t_ref, blocks, base, keys, values, peak):
    inner = weight_ref.shape[1] // 4
    heads, depth = values.shape[0], values.shape[1]
    head_size = inner // heads

    def step(block, peak):
        source = pl.ds(pl.multiple_of(block * BLOCK, BLOCK), BLOCK)
        place = pl.ds(pl.multiple_of(base + block * BLOCK, BLOCK), BLOCK)
        part = packed[source, :]
        key_part = jnp.dot(
            part, weight_ref[:, inner : 2 * inner], preferred_element_type=jnp.float32
        )
        turned = lax.dot_general(
            weight_t_ref[2 * inner : 3 * inner, :], part, NT, preferred_element_type=jnp.float32
        ).astype(jnp.bfloat16)
        keys[place, :] = key_part.astype(jnp.bfloat16)
        for h in range(heads):
            values[h, 0:head_size, place] = turned[h * head_size : (h + 1) * head_size]
            values[h, head_size:, place] = jnp.ones((depth - head_size, BLOCK), jnp.bfloat16)
        return jnp.maximum(
            peak, jnp.max(jnp.abs(key_part).reshape(BLOCK // 8, 8, inner), axis=0)
        )

    return lax.fori_loop(0, blocks, step, peak)


def near_kernel(
    valid_ref,
    own_ref,
    sides_ref,
    across_ref,
    left_own_ref,
    left_sides_ref,
    left_across_ref,
    right_own_ref,
    right_sides_ref,
    right_across_ref,
    weight_ref,
    weight_t_ref,
    keys_ref,
    values_ref,
    queries_ref,
    gates_ref,
    peaks_ref,
    packed,
    table,
):
    heads = queries_ref.shape[0]
    inner = queries_ref.shape[2]
    head_size = inner // heads
    own = own_ref[0, 0]
    turned = lax.dot_general(weight_t_ref[0:inner, :], own, NT, preferred_element_type=jnp.float32)
    turned = (turned * head_size ** (-0.5)).astype(jnp.bfloat16)
    gate = jax.nn.sigmoid(
        lax.dot_general(
            weight_t_ref[3 * inner : 4 * inner, :], own, NT, preferred_element_type=jnp.float32
        )
    )
    queries_ref[...] = jnp.zeros_like(queries_ref)
    for h in range(heads):
        span = slice(h * head_size, (h + 1) * head_size)
        queries_ref[h, 0, span, :] = turned[span]
        gates_ref[h, 0] = gate[span]
    places = range(NEAR)

    @pl.when(pl.program_id(0) == 0)
    def _():
        chart(valid_ref, table, places)

    refs = (
        own_ref,
        sides_ref,
        across_ref,
        left_own_ref,
        left_sides_ref,
        left_across_ref,
        right_own_ref,
        right_sides_ref,
        right_across_ref,
    )
    pack(table, places, refs, 0, packed)
    blocks = (table[2, 0] + (BLOCK - 1)) >> 8
    peaks_ref[0] = project(
        packed,
        weight_ref,
        weight_t_ref,
        blocks,
        0,
        keys_ref.at[0],
        values_ref.at[0],
        jnp.zeros((8, inner), jnp.float32),
    )


def piece_spec(piece):
    count, _, cols, width = piece.shape
    return pl.BlockSpec((count, 1, cols, width), lambda i: (0, i, 0, 0))


def fixed(array):
    zeros = (0,) * array.ndim
    return pl.BlockSpec(array.shape, lambda i: zeros, pipeline_mode=pl.Buffered(1))


def project_near(chain_valid, pieces, weight, weight_t, heads):
    _, rows, cols, width = pieces[0].shape
    inner = weight.shape[1] // 4
    head_size = inner // heads
    depth = head_size + GROUP
    return pl.pallas_call(
        near_kernel,
        grid=(rows,),
        in_specs=[
            SMEM,
            *(piece_spec(piece) for piece in pieces),
            fixed(weight),
            fixed(weight_t),
        ],
        out_specs=(
            pl.BlockSpec((1, NEAR_ROOM, inner), lambda i: (i, 0, 0)),
            pl.BlockSpec((1, heads, depth, NEAR_ROOM), lambda i: (i, 0, 0, 0)),
            pl.BlockSpec((heads, 1, inner, cols), lambda i: (0, i, 0, 0)),
            pl.BlockSpec((heads, 1, head_size, cols), lambda i: (0, i, 0, 0)),
            pl.BlockSpec((1, 8, inner), lambda i: (i, 0, 0)),
        ),
        out_shape=(
            jax.ShapeDtypeStruct((rows, NEAR_ROOM, inner), jnp.bfloat16),
            jax.ShapeDtypeStruct((rows, heads, depth, NEAR_ROOM), jnp.bfloat16),
            jax.ShapeDtypeStruct((heads, rows, inner, cols), jnp.bfloat16),
            jax.ShapeDtypeStruct((heads, rows, head_size, cols), jnp.float32),
            jax.ShapeDtypeStruct((rows, 8, inner), jnp.float32),
        ),
        scratch_shapes=[
            pltpu.VMEM((NEAR * SLOT + BLOCK, width), jnp.bfloat16),
            pltpu.SMEM((3, NEAR + FAR), jnp.int32),
        ],
        name="near",
    )(chain_valid, *pieces, weight, weight_t)


def attend_kernel(
    valid_ref,
    keys_hbm,
    values_hbm,
    low_ref,
    high_ref,
    weight_ref,
    weight_t_ref,
    queries,
    peaks_ref,
    gates,
    bias_ref,
    out_weight_ref,
    out_ref,
    keys,
    values,
    packed,
    gated,
    bias,
    shifted,
    sums,
    table,
    safe,
    sems,
):
    heads, rows, inner, cols = queries.shape
    head_size = inner // heads
    head = pl.program_id(0)
    half = bias_ref.shape[0]
    y_low = lax.axis_index("rows") >> 4
    spans = ((0, range(NEAR)), (NEAR_ROOM, range(NEAR, NEAR + FAR)))
    key_copy = pltpu.make_async_copy(keys_hbm, keys.at[:, pl.ds(0, NEAR_ROOM), :], sems.at[heads])

    def value_copy(h):
        return pltpu.make_async_copy(
            values_hbm.at[:, h], values.at[:, h, :, pl.ds(0, NEAR_ROOM)], sems.at[h]
        )

    @pl.when(head == 0)
    def _():
        key_copy.start()
        for h in range(heads):
            value_copy(h).start()
        for _, places in spans:
            chart(valid_ref, table, places)
        far = range(NEAR, NEAR + FAR)
        blocks = (table[2, NEAR] + (BLOCK - 1)) >> 8
        best = jnp.float32(0.0)
        for row in range(rows):
            pack(table, far, (low_ref, high_ref), row, packed)
            peak = project(
                packed,
                weight_ref,
                weight_t_ref,
                blocks,
                NEAR_ROOM,
                keys.at[row],
                values.at[row],
                peaks_ref[row],
            )
            peak = jnp.max(peak, axis=0, keepdims=True)
            peak = jnp.transpose(jnp.broadcast_to(peak, (inner, inner)))[:, 0:1]
            for h in range(heads):
                span = slice(h * head_size, (h + 1) * head_size)
                spread = jnp.abs(queries[h, row, span, :].astype(jnp.float32)) * peak[span]
                best = jnp.maximum(best, jnp.max(jnp.sum(spread, axis=0, keepdims=True)))
        safe[0] = (best < REACH).astype(jnp.int32)
        key_copy.wait()

    for h in range(heads):

        @pl.when(head == h)
        def _(h=h):
            value_copy(h).wait()

    top = jnp.full((GROUP, cols), MASKED, jnp.bfloat16)
    counts = []
    for base, places in spans:
        total = table[2, places[0]]

        def move(place, top, base=base):
            start, chain = table[0, place], table[1, place]
            piece = bias_ref[chain & (half - 1), (chain >> 4) ^ y_low, 0]
            bias[pl.ds(pl.multiple_of(base + start, GROUP), SLOT), :] = piece
            for group in range(0, SLOT, GROUP):
                top = jnp.maximum(top, piece[group : group + GROUP])
            return top

        top = lax.fori_loop(places[0], places[-1] + 1, move, top)
        bias[pl.ds(pl.multiple_of(base + total, GROUP), BLOCK), :] = jnp.full(
            (BLOCK, cols), MASKED, jnp.bfloat16
        )
        counts.append((total + (BLOCK - 1)) >> 8)
    near_blocks, blocks = counts[0], counts[0] + counts[1]
    top = jnp.max(top.astype(jnp.float32), axis=0, keepdims=True)
    sums[...] = jnp.zeros_like(sums)

    def place_of(block):
        block = jnp.where(block < near_blocks, block, block - near_blocks + NEAR_ROOM // BLOCK)
        return pl.ds(pl.multiple_of(block * BLOCK, BLOCK), BLOCK)

    @pl.when(safe[0] == 1)
    def _():
        def span(first, count):
            parts = [place_of(first + n) for n in range(count)]
            for n, place in enumerate(parts):
                shifted[n] = (bias[place, :].astype(jnp.float32) - top) * LOG2E
            weights = []
            for n, place in enumerate(parts):
                scores = [
                    jnp.dot(keys[row, place, :], queries[head, row], preferred_element_type=jnp.float32) for row in range(rows)
                ]
                weights.append(
                    [jnp.exp2(part * LOG2E + shifted[n]).astype(jnp.bfloat16) for part in scores]
                )
            for n, place in enumerate(parts):
                for row in range(rows):
                    sums[row] += jnp.dot(
                        values[row, head, :, place], weights[n][row], preferred_element_type=jnp.float32
                    )

        def double(pair, carry):
            span(2 * pair, 2)
            return carry

        lax.fori_loop(0, blocks >> 1, double, 0)

        @pl.when((blocks & 1) == 1)
        def _():
            span(blocks - 1, 1)

    @pl.when(safe[0] == 0)
    def _():
        def step(block, state):
            place = place_of(block)
            bias_block = bias[place, :].astype(jnp.float32)
            fresh = []
            for row in range(rows):
                scores = jnp.dot(
                    keys[row, place, :], queries[head, row], preferred_element_type=jnp.float32
                )
                scores = scores + bias_block
                new_max = jnp.maximum(state[row], jnp.max(scores, axis=0, keepdims=True))
                weights = jnp.exp(scores - new_max).astype(jnp.bfloat16)
                weighted = jnp.dot(
                    values[row, head, :, place], weights, preferred_element_type=jnp.float32
                )
                sums[row] = sums[row] * jnp.exp(state[row] - new_max) + weighted
                fresh.append(new_max)
            return tuple(fresh)

        lax.fori_loop(
            0,
            blocks,
            step,
            tuple(jnp.full((1, cols), -jnp.inf, jnp.float32) for _ in range(rows)),
        )

    for row in range(rows):
        total_row = sums[row]
        attended = total_row[0:head_size] / total_row[head_size : head_size + 1]
        gated[row, pl.ds(pl.multiple_of(head * head_size, head_size), head_size), :] = (
            attended * gates[0, row]
        ).astype(jnp.bfloat16)

    @pl.when(head == heads - 1)
    def _():
        for row in range(rows):
            out_ref[row] = lax.dot_general(
                gated[row], out_weight_ref[...], TN, preferred_element_type=jnp.float32
            ).astype(jnp.bfloat16)


def attend(
    chain_valid, keys, values, far, weight, weight_t, queries, peaks, gates, bias, output_weight
):
    heads, rows, inner, cols = queries.shape
    depth = values.shape[2]
    half, pair, _, slot, _ = bias.shape
    width = output_weight.shape[1]
    return pl.pallas_call(
        attend_kernel,
        grid=(heads,),
        in_specs=[
            SMEM,
            pl.BlockSpec(memory_space=pl.ANY),
            pl.BlockSpec(memory_space=pl.ANY),
            *(fixed(piece) for piece in far),
            fixed(weight),
            fixed(weight_t),
            fixed(queries),
            fixed(peaks),
            pl.BlockSpec((1, rows, inner // heads, cols), lambda h: (h, 0, 0, 0)),
            pl.BlockSpec((half, pair, 1, slot, cols), lambda h: (0, 0, h, 0, 0)),
            fixed(output_weight),
        ],
        out_specs=pl.BlockSpec((rows, cols, width), lambda h: (0, 0, 0)),
        scratch_shapes=[
            pltpu.VMEM((rows, ROOM, inner), jnp.bfloat16),
            pltpu.VMEM((rows, heads, depth, ROOM), jnp.bfloat16),
            pltpu.VMEM((FAR_ROOM, weight.shape[0]), jnp.bfloat16),
            pltpu.VMEM((rows, inner, cols), jnp.bfloat16),
            pltpu.VMEM((ROOM, cols), jnp.bfloat16),
            pltpu.VMEM((2, BLOCK, cols), jnp.float32),
            pltpu.VMEM((rows, depth, cols), jnp.float32),
            pltpu.SMEM((3, NEAR + FAR), jnp.int32),
            pltpu.SMEM((1,), jnp.int32),
            pltpu.SemaphoreType.DMA((heads + 1,)),
        ],
        out_shape=jax.ShapeDtypeStruct((rows, cols, width), jnp.bfloat16),
        name="attend",
    )(
        chain_valid,
        keys,
        values,
        *far,
        weight,
        weight_t,
        queries,
        peaks,
        gates,
        bias,
        output_weight,
    )


def shift(value, x_step, y_step):
    pairs = [
        (x * YS + y, (x + x_step) % XS * YS + (y + y_step) % YS)
        for x in range(XS)
        for y in range(YS)
    ]
    return lax.ppermute(value, "cols", pairs)


def gather_bias(bias_t):
    count = lax.axis_size("rows")
    half = count // 2
    swapped = lax.ppermute(bias_t, "rows", [(r, (r + half) % count) for r in range(count)])
    both = jnp.stack([bias_t, swapped])
    groups = [list(range(half)), list(range(half, count))]
    return lax.all_gather(both, "rows", axis_index_groups=groups)


def finish(chain_valid, near, far, bias, project_weight, output_weight, heads):
    weight_t = project_weight.T
    keys, values, queries, gates, peaks = project_near(
        chain_valid, near, project_weight, weight_t, heads
    )
    return attend(
        chain_valid,
        keys,
        values,
        far,
        project_weight,
        weight_t,
        queries,
        peaks,
        gates,
        bias,
        output_weight,
    )


def local(pair_rep, project_weight, output_weight, pair_bias, chain_valid):
    normed, bias_t = prep(pair_rep, pair_bias, chain_valid)
    bias = gather_bias(bias_t)
    left_own = shift(normed, 1, 0)
    right_own = shift(normed, -1, 0)
    above = shift(normed, 0, 1)
    below = shift(normed, 0, -1)
    across = shift(normed, 0, 2)
    sides = jnp.stack([above, below])
    left_sides = shift(sides, 1, 0)
    right_sides = shift(sides, -1, 0)
    left_across = shift(across, 1, 0)
    right_across = shift(across, -1, 0)
    far_low = shift(jnp.stack([left_own, left_sides[0]]), 1, 0)
    far_high = shift(jnp.stack([right_sides[1], right_across]), -1, 0)
    near = (
        normed[None],
        sides,
        across[None],
        left_own[None],
        left_sides,
        left_across[None],
        right_own[None],
        right_sides,
        right_across[None],
    )
    return finish(
        chain_valid,
        near,
        (far_low, far_high),
        bias,
        project_weight,
        output_weight,
        pair_bias.shape[0],
    )


def solution(mesh):
    return jax.shard_map(
        local,
        mesh=mesh,
        in_specs=(P("rows", "cols", None), P(), P(), P(None, "cols", "rows"), P()),
        out_specs=P("rows", "cols", None),
        check_vma=False,
    )
```

```python
import jax
import jax.numpy as jnp
from jax import lax
from jax.experimental import pallas as pl
from jax.experimental.pallas import tpu as pltpu
from jax.sharding import PartitionSpec as P


SLOT = 128
GROUP = 16
BLOCK = 256
MASKED = -1000000000.0
LOG2E = 1.4426950408889634
REACH = 60.0
XS, YS = 4, 4
PER_COL = 2
NEAR = 12 * PER_COL
FAR = 4 * PER_COL
NEAR_ROOM = NEAR * SLOT + BLOCK
FAR_ROOM = FAR * SLOT + BLOCK
ROOM = NEAR_ROOM + FAR_ROOM

NT = (((1,), (1,)), ((), ()))
TN = (((0,), (0,)), ((), ()))

SMEM = pl.BlockSpec(memory_space=pltpu.SMEM)
VMEM = pl.BlockSpec(memory_space=pltpu.VMEM)


def prep_kernel(valid_ref, pair_ref, bias_ref, normed_ref, biast_ref):
    pair = pair_ref[...].astype(jnp.float32)
    center = jnp.mean(pair, axis=-1, keepdims=True)
    spread = jnp.mean(jnp.square(pair - center), axis=-1, keepdims=True)
    normed_ref[...] = ((pair - center) * lax.rsqrt(spread + 1e-05)).astype(jnp.bfloat16)
    heads, queries, keys = bias_ref.shape
    valid = valid_ref[lax.axis_index("rows")]
    live = lax.broadcasted_iota(jnp.int32, (keys, queries), 0) < valid
    for head in range(heads):
        turned = jnp.transpose(bias_ref[head].astype(jnp.float32))
        biast_ref[head] = jnp.where(live, turned, MASKED).astype(jnp.bfloat16)


def prep(pair_rep, pair_bias, chain_valid):
    heads, queries, keys = pair_bias.shape
    return pl.pallas_call(
        prep_kernel,
        out_shape=(
            jax.ShapeDtypeStruct(pair_rep.shape, jnp.bfloat16),
            jax.ShapeDtypeStruct((heads, keys, queries), jnp.bfloat16),
        ),
        in_specs=[SMEM, VMEM, VMEM],
        out_specs=(VMEM, VMEM),
        name="prep",
    )(chain_valid, pair_rep, pair_bias)


def chart(valid_ref, table, places):
    col = lax.axis_index("cols")
    x, y = col >> 2, col & 3
    total = jnp.int32(0)
    for place in places:
        x_step = (0, 3, 1, 2)[place // (YS * PER_COL)]
        y_step = (0, 3, 1, 2)[place // PER_COL % YS]
        from_col = ((x + x_step) & (XS - 1)) * YS + ((y + y_step) & (YS - 1))
        chain = from_col * PER_COL + place % PER_COL
        table[0, place] = total
        table[1, place] = chain
        total = total + ((valid_ref[chain] + (GROUP - 1)) >> 4 << 4)
    table[2, places[0]] = total


def pack(table, places, refs, row, packed):
    sources = [
        (ref, piece, part)
        for ref in refs
        for piece in range(ref.shape[0])
        for part in range(PER_COL)
    ]
    total = table[2, places[0]]
    for (ref, piece, part), place in zip(sources, places):
        packed[pl.ds(pl.multiple_of(table[0, place], GROUP), SLOT), :] = ref[
            piece, row, part * SLOT : (part + 1) * SLOT, :
        ]
    packed[pl.ds(pl.multiple_of(total, GROUP), BLOCK), :] = jnp.zeros(
        (BLOCK, packed.shape[1]), jnp.bfloat16
    )


def project(packed, weight_ref, weight_t_ref, blocks, base, keys, values, peak):
    inner = weight_ref.shape[1] // 4
    heads, depth = values.shape[0], values.shape[1]
    head_size = inner // heads

    def step(block, peak):
        source = pl.ds(pl.multiple_of(block * BLOCK, BLOCK), BLOCK)
        place = pl.ds(pl.multiple_of(base + block * BLOCK, BLOCK), BLOCK)
        part = packed[source, :]
        key_part = jnp.dot(
            part, weight_ref[:, inner : 2 * inner], preferred_element_type=jnp.float32
        )
        turned = lax.dot_general(
            weight_t_ref[2 * inner : 3 * inner, :], part, NT, preferred_element_type=jnp.float32
        ).astype(jnp.bfloat16)
        keys[place, :] = key_part.astype(jnp.bfloat16)
        for h in range(heads):
            values[h, 0:head_size, place] = turned[h * head_size : (h + 1) * head_size]
            values[h, head_size:, place] = jnp.ones((depth - head_size, BLOCK), jnp.bfloat16)
        return jnp.maximum(
            peak, jnp.max(jnp.abs(key_part).reshape(BLOCK // 8, 8, inner), axis=0)
        )

    return lax.fori_loop(0, blocks, step, peak)


def near_kernel(
    valid_ref,
    own_ref,
    sides_ref,
    across_ref,
    left_own_ref,
    left_sides_ref,
    left_across_ref,
    right_own_ref,
    right_sides_ref,
    right_across_ref,
    weight_ref,
    weight_t_ref,
    keys_ref,
    values_ref,
    queries_ref,
    gates_ref,
    peaks_ref,
    packed,
    table,
):
    heads = queries_ref.shape[0]
    inner = queries_ref.shape[2]
    head_size = inner // heads
    own = own_ref[0, 0]
    turned = lax.dot_general(weight_t_ref[0:inner, :], own, NT, preferred_element_type=jnp.float32)
    turned = (turned * head_size ** (-0.5)).astype(jnp.bfloat16)
    gate = jax.nn.sigmoid(
        lax.dot_general(
            weight_t_ref[3 * inner : 4 * inner, :], own, NT, preferred_element_type=jnp.float32
        )
    )
    queries_ref[...] = jnp.zeros_like(queries_ref)
    for h in range(heads):
        span = slice(h * head_size, (h + 1) * head_size)
        queries_ref[h, 0, span, :] = turned[span]
        gates_ref[h, 0] = gate[span]
    places = range(NEAR)

    @pl.when(pl.program_id(0) == 0)
    def _():
        chart(valid_ref, table, places)

    refs = (
        own_ref,
        sides_ref,
        across_ref,
        left_own_ref,
        left_sides_ref,
        left_across_ref,
        right_own_ref,
        right_sides_ref,
        right_across_ref,
    )
    pack(table, places, refs, 0, packed)
    blocks = (table[2, 0] + (BLOCK - 1)) >> 8
    peaks_ref[0] = project(
        packed,
        weight_ref,
        weight_t_ref,
        blocks,
        0,
        keys_ref.at[0],
        values_ref.at[0],
        jnp.zeros((8, inner), jnp.float32),
    )


def far_kernel(
    valid_ref,
    low_ref,
    high_ref,
    weight_ref,
    weight_t_ref,
    queries_ref,
    peaks_ref,
    keys_ref,
    values_ref,
    safe_ref,
    packed,
    table,
    reach,
):
    row = pl.program_id(0)
    heads, _, inner, _ = queries_ref.shape
    head_size = inner // heads
    places = range(NEAR, NEAR + FAR)

    @pl.when(row == 0)
    def _():
        chart(valid_ref, table, places)
        reach[0] = jnp.float32(0.0)

    pack(table, places, (low_ref, high_ref), 0, packed)
    blocks = (table[2, NEAR] + (BLOCK - 1)) >> 8
    peak = project(
        packed,
        weight_ref,
        weight_t_ref,
        blocks,
        0,
        keys_ref.at[0],
        values_ref.at[0],
        peaks_ref[0],
    )
    peak = jnp.max(peak, axis=0, keepdims=True)
    peak = jnp.transpose(jnp.broadcast_to(peak, (inner, inner)))[:, 0:1]
    best = reach[0]
    for h in range(heads):
        span = slice(h * head_size, (h + 1) * head_size)
        spread = jnp.abs(queries_ref[h, 0, span, :].astype(jnp.float32)) * peak[span]
        best = jnp.maximum(best, jnp.max(jnp.sum(spread, axis=0, keepdims=True)))
    reach[0] = best
    safe_ref[0] = (best < REACH).astype(jnp.int32)


def piece_spec(piece):
    count, _, cols, width = piece.shape
    return pl.BlockSpec((count, 1, cols, width), lambda i: (0, i, 0, 0))


def fixed(array):
    zeros = (0,) * array.ndim
    return pl.BlockSpec(array.shape, lambda i: zeros, pipeline_mode=pl.Buffered(1))


def project_near(chain_valid, pieces, weight, weight_t, heads):
    _, rows, cols, width = pieces[0].shape
    inner = weight.shape[1] // 4
    head_size = inner // heads
    depth = head_size + GROUP
    return pl.pallas_call(
        near_kernel,
        grid=(rows,),
        in_specs=[
            SMEM,
            *(piece_spec(piece) for piece in pieces),
            fixed(weight),
            fixed(weight_t),
        ],
        out_specs=(
            pl.BlockSpec((1, NEAR_ROOM, inner), lambda i: (i, 0, 0)),
            pl.BlockSpec((1, heads, depth, NEAR_ROOM), lambda i: (i, 0, 0, 0)),
            pl.BlockSpec((heads, 1, inner, cols), lambda i: (0, i, 0, 0)),
            pl.BlockSpec((heads, 1, head_size, cols), lambda i: (0, i, 0, 0)),
            pl.BlockSpec((1, 8, inner), lambda i: (i, 0, 0)),
        ),
        out_shape=(
            jax.ShapeDtypeStruct((rows, NEAR_ROOM, inner), jnp.bfloat16),
            jax.ShapeDtypeStruct((rows, heads, depth, NEAR_ROOM), jnp.bfloat16),
            jax.ShapeDtypeStruct((heads, rows, inner, cols), jnp.bfloat16),
            jax.ShapeDtypeStruct((heads, rows, head_size, cols), jnp.float32),
            jax.ShapeDtypeStruct((rows, 8, inner), jnp.float32),
        ),
        scratch_shapes=[
            pltpu.VMEM((NEAR * SLOT + BLOCK, width), jnp.bfloat16),
            pltpu.SMEM((3, NEAR + FAR), jnp.int32),
        ],
        name="near",
    )(chain_valid, *pieces, weight, weight_t)


def project_far(chain_valid, pieces, weight, weight_t, queries, peaks, depth):
    heads, rows, inner, cols = queries.shape
    width = weight.shape[0]
    return pl.pallas_call(
        far_kernel,
        grid=(rows,),
        in_specs=[
            SMEM,
            *(piece_spec(piece) for piece in pieces),
            fixed(weight),
            fixed(weight_t),
            pl.BlockSpec((heads, 1, inner, cols), lambda i: (0, i, 0, 0)),
            pl.BlockSpec((1, 8, inner), lambda i: (i, 0, 0)),
        ],
        out_specs=(
            pl.BlockSpec((1, FAR_ROOM, inner), lambda i: (i, 0, 0)),
            pl.BlockSpec((1, heads, depth, FAR_ROOM), lambda i: (i, 0, 0, 0)),
            SMEM,
        ),
        out_shape=(
            jax.ShapeDtypeStruct((rows, FAR_ROOM, inner), jnp.bfloat16),
            jax.ShapeDtypeStruct((rows, heads, depth, FAR_ROOM), jnp.bfloat16),
            jax.ShapeDtypeStruct((1,), jnp.int32),
        ),
        scratch_shapes=[
            pltpu.VMEM((FAR_ROOM, width), jnp.bfloat16),
            pltpu.SMEM((3, NEAR + FAR), jnp.int32),
            pltpu.SMEM((1,), jnp.float32),
        ],
        name="far",
    )(chain_valid, *pieces, weight, weight_t, queries, peaks)


def attend_kernel(
    valid_ref,
    safe,
    near_keys,
    near_values,
    far_keys,
    far_values,
    queries,
    gates,
    bias_ref,
    out_weight_ref,
    out_ref,
    keys,
    values,
    gated,
    bias,
    shifted,
    sums,
    table,
    sems,
):
    heads, rows, inner, cols = queries.shape
    head_size = inner // heads
    head = pl.program_id(0)
    half = bias_ref.shape[0]
    y_low = lax.axis_index("rows") >> 4
    spans = ((0, range(NEAR)), (NEAR_ROOM, range(NEAR, NEAR + FAR)))
    near_room, far_room = pl.ds(0, NEAR_ROOM), pl.ds(NEAR_ROOM, FAR_ROOM)
    key_copies = (
        pltpu.make_async_copy(near_keys, keys.at[:, near_room, :], sems.at[0, heads]),
        pltpu.make_async_copy(far_keys, keys.at[:, far_room, :], sems.at[1, heads]),
    )

    def value_copies(h):
        return (
            pltpu.make_async_copy(
                near_values.at[:, h], values.at[:, h, :, near_room], sems.at[0, h]
            ),
            pltpu.make_async_copy(far_values.at[:, h], values.at[:, h, :, far_room], sems.at[1, h]),
        )

    @pl.when(head == 0)
    def _():
        for copy in key_copies + value_copies(0):
            copy.start()
        for _, places in spans:
            chart(valid_ref, table, places)

    top = jnp.full((GROUP, cols), MASKED, jnp.bfloat16)
    counts = []
    for base, places in spans:
        total = table[2, places[0]]

        def move(place, top, base=base):
            start, chain = table[0, place], table[1, place]
            piece = bias_ref[chain & (half - 1), (chain >> 4) ^ y_low, 0]
            bias[pl.ds(pl.multiple_of(base + start, GROUP), SLOT), :] = piece
            for group in range(0, SLOT, GROUP):
                top = jnp.maximum(top, piece[group : group + GROUP])
            return top

        top = lax.fori_loop(places[0], places[-1] + 1, move, top, unroll=4)
        bias[pl.ds(pl.multiple_of(base + total, GROUP), BLOCK), :] = jnp.full(
            (BLOCK, cols), MASKED, jnp.bfloat16
        )
        counts.append((total + (BLOCK - 1)) >> 8)

    @pl.when(head == 0)
    def _():
        for copy in key_copies:
            copy.wait()
        for h in range(1, heads):
            for copy in value_copies(h):
                copy.start()

    for h in range(heads):

        @pl.when(head == h)
        def _(h=h):
            for copy in value_copies(h):
                copy.wait()

    near_blocks, blocks = counts[0], counts[0] + counts[1]
    top = jnp.max(top.astype(jnp.float32), axis=0, keepdims=True)
    sums[...] = jnp.zeros_like(sums)

    def place_of(block):
        block = jnp.where(block < near_blocks, block, block - near_blocks + NEAR_ROOM // BLOCK)
        return pl.ds(pl.multiple_of(block * BLOCK, BLOCK), BLOCK)

    @pl.when(safe[0] == 1)
    def _():
        def span(first, count):
            parts = [place_of(first + n) for n in range(count)]
            for n, place in enumerate(parts):
                shifted[n] = (bias[place, :].astype(jnp.float32) - top) * LOG2E
            weights = []
            for n, place in enumerate(parts):
                scores = [
                    jnp.dot(keys[row, place, :], queries[head, row], preferred_element_type=jnp.float32) for row in range(rows)
                ]
                weights.append(
                    [jnp.exp2(part * LOG2E + shifted[n]).astype(jnp.bfloat16) for part in scores]
                )
            for n, place in enumerate(parts):
                for row in range(rows):
                    sums[row] += jnp.dot(
                        values[row, head, :, place], weights[n][row], preferred_element_type=jnp.float32
                    )

        def double(pair, carry):
            span(2 * pair, 2)
            return carry

        lax.fori_loop(0, blocks >> 1, double, 0)

        @pl.when((blocks & 1) == 1)
        def _():
            span(blocks - 1, 1)

    @pl.when(safe[0] == 0)
    def _():
        def step(block, state):
            place = place_of(block)
            bias_block = bias[place, :].astype(jnp.float32)
            fresh = []
            for row in range(rows):
                scores = jnp.dot(
                    keys[row, place, :], queries[head, row], preferred_element_type=jnp.float32
                )
                scores = scores + bias_block
                new_max = jnp.maximum(state[row], jnp.max(scores, axis=0, keepdims=True))
                weights = jnp.exp(scores - new_max).astype(jnp.bfloat16)
                weighted = jnp.dot(
                    values[row, head, :, place], weights, preferred_element_type=jnp.float32
                )
                sums[row] = sums[row] * jnp.exp(state[row] - new_max) + weighted
                fresh.append(new_max)
            return tuple(fresh)

        lax.fori_loop(
            0,
            blocks,
            step,
            tuple(jnp.full((1, cols), -jnp.inf, jnp.float32) for _ in range(rows)),
        )

    for row in range(rows):
        total_row = sums[row]
        attended = total_row[0:head_size] / total_row[head_size : head_size + 1]
        gated[row, pl.ds(pl.multiple_of(head * head_size, head_size), head_size), :] = (
            attended * gates[0, row]
        ).astype(jnp.bfloat16)

    @pl.when(head == heads - 1)
    def _():
        for row in range(rows):
            out_ref[row] = lax.dot_general(
                gated[row], out_weight_ref[...], TN, preferred_element_type=jnp.float32
            ).astype(jnp.bfloat16)


def attend(
    chain_valid,
    safe,
    near_keys,
    near_values,
    far_keys,
    far_values,
    queries,
    gates,
    bias,
    output_weight,
):
    heads, rows, inner, cols = queries.shape
    depth = near_values.shape[2]
    half, pair, _, slot, _ = bias.shape
    width = output_weight.shape[1]
    return pl.pallas_call(
        attend_kernel,
        grid=(heads,),
        in_specs=[
            SMEM,
            SMEM,
            *[pl.BlockSpec(memory_space=pl.ANY)] * 4,
            fixed(queries),
            pl.BlockSpec((1, rows, inner // heads, cols), lambda h: (h, 0, 0, 0)),
            pl.BlockSpec((half, pair, 1, slot, cols), lambda h: (0, 0, h, 0, 0)),
            fixed(output_weight),
        ],
        out_specs=pl.BlockSpec((rows, cols, width), lambda h: (0, 0, 0)),
        scratch_shapes=[
            pltpu.VMEM((rows, ROOM, inner), jnp.bfloat16),
            pltpu.VMEM((rows, heads, depth, ROOM), jnp.bfloat16),
            pltpu.VMEM((rows, inner, cols), jnp.bfloat16),
            pltpu.VMEM((ROOM, cols), jnp.bfloat16),
            pltpu.VMEM((2, BLOCK, cols), jnp.float32),
            pltpu.VMEM((rows, depth, cols), jnp.float32),
            pltpu.SMEM((3, NEAR + FAR), jnp.int32),
            pltpu.SemaphoreType.DMA((2, heads + 1)),
        ],
        out_shape=jax.ShapeDtypeStruct((rows, cols, width), jnp.bfloat16),
        name="attend",
    )(
        chain_valid,
        safe,
        near_keys,
        near_values,
        far_keys,
        far_values,
        queries,
        gates,
        bias,
        output_weight,
    )


def shift(value, x_step, y_step):
    pairs = [
        (x * YS + y, (x + x_step) % XS * YS + (y + y_step) % YS)
        for x in range(XS)
        for y in range(YS)
    ]
    return lax.ppermute(value, "cols", pairs)


def gather_bias(bias_t):
    count = lax.axis_size("rows")
    half = count // 2
    swapped = lax.ppermute(bias_t, "rows", [(r, (r + half) % count) for r in range(count)])
    both = jnp.stack([bias_t, swapped])
    groups = [list(range(half)), list(range(half, count))]
    return lax.all_gather(both, "rows", axis_index_groups=groups)


def finish(chain_valid, near, far, bias, project_weight, output_weight, heads):
    weight_t = project_weight.T
    keys, values, queries, gates, peaks = project_near(
        chain_valid, near, project_weight, weight_t, heads
    )
    far_keys, far_values, safe = project_far(
        chain_valid, far, project_weight, weight_t, queries, peaks, values.shape[2]
    )
    return attend(
        chain_valid,
        safe,
        keys,
        values,
        far_keys,
        far_values,
        queries,
        gates,
        bias,
        output_weight,
    )


def local(pair_rep, project_weight, output_weight, pair_bias, chain_valid):
    normed, bias_t = prep(pair_rep, pair_bias, chain_valid)
    bias = gather_bias(bias_t)
    left_own = shift(normed, 1, 0)
    right_own = shift(normed, -1, 0)
    above = shift(normed, 0, 1)
    below = shift(normed, 0, -1)
    half = normed.shape[0] // 2
    across_low = shift(above[:half], 0, 1)
    across_high = shift(below[half:], 0, -1)
    across = jnp.concatenate([across_low, across_high])
    sides = jnp.stack([above, below])
    left_sides = shift(sides, 1, 0)
    right_sides = shift(sides, -1, 0)
    left_across = shift(across, 1, 0)
    right_across = shift(across, -1, 0)
    far_low = shift(jnp.stack([left_own, left_sides[0]]), 1, 0)
    far_high = shift(jnp.stack([right_sides[1], right_across]), -1, 0)
    near = (
        normed[None],
        sides,
        across[None],
        left_own[None],
        left_sides,
        left_across[None],
        right_own[None],
        right_sides,
        right_across[None],
    )
    return finish(
        chain_valid,
        near,
        (far_low, far_high),
        bias,
        project_weight,
        output_weight,
        pair_bias.shape[0],
    )


def solution(mesh):
    return jax.shard_map(
        local,
        mesh=mesh,
        in_specs=(P("rows", "cols", None), P(), P(), P(None, "cols", "rows"), P()),
        out_specs=P("rows", "cols", None),
        check_vma=False,
    )
```

```python
import jax
import jax.numpy as jnp
from jax import lax
from jax.experimental import pallas as pl
from jax.experimental.pallas import tpu as pltpu
from jax.sharding import PartitionSpec as P


SLOT = 128
GROUP = 16
BLOCK = 256
MASKED = -1000000000.0
LOG2E = 1.4426950408889634
REACH = 60.0
XS, YS = 4, 4
PER_COL = 2
NEAR = 12 * PER_COL
FAR = 4 * PER_COL
NEAR_ROOM = NEAR * SLOT + BLOCK
FAR_ROOM = FAR * SLOT + BLOCK
ROOM = NEAR_ROOM + FAR_ROOM

NT = (((1,), (1,)), ((), ()))
TN = (((0,), (0,)), ((), ()))

SMEM = pl.BlockSpec(memory_space=pltpu.SMEM)
VMEM = pl.BlockSpec(memory_space=pltpu.VMEM)


def prep_kernel(valid_ref, pair_ref, bias_ref, normed_ref, biast_ref):
    pair = pair_ref[...].astype(jnp.float32)
    center = jnp.mean(pair, axis=-1, keepdims=True)
    spread = jnp.mean(jnp.square(pair - center), axis=-1, keepdims=True)
    normed_ref[...] = ((pair - center) * lax.rsqrt(spread + 1e-05)).astype(jnp.bfloat16)
    heads, queries, keys = bias_ref.shape
    valid = valid_ref[lax.axis_index("rows")]
    live = lax.broadcasted_iota(jnp.int32, (keys, queries), 0) < valid
    for head in range(heads):
        turned = jnp.transpose(bias_ref[head].astype(jnp.float32))
        biast_ref[head] = jnp.where(live, turned, MASKED).astype(jnp.bfloat16)


def prep(pair_rep, pair_bias, chain_valid):
    heads, queries, keys = pair_bias.shape
    return pl.pallas_call(
        prep_kernel,
        out_shape=(
            jax.ShapeDtypeStruct(pair_rep.shape, jnp.bfloat16),
            jax.ShapeDtypeStruct((heads, keys, queries), jnp.bfloat16),
        ),
        in_specs=[SMEM, VMEM, VMEM],
        out_specs=(VMEM, VMEM),
        name="prep",
    )(chain_valid, pair_rep, pair_bias)


def chart(valid_ref, table, places):
    col = lax.axis_index("cols")
    x, y = col >> 2, col & 3
    total = jnp.int32(0)
    for place in places:
        x_step = (0, 3, 1, 2)[place // (YS * PER_COL)]
        y_step = (0, 3, 1, 2)[place // PER_COL % YS]
        from_col = ((x + x_step) & (XS - 1)) * YS + ((y + y_step) & (YS - 1))
        chain = from_col * PER_COL + place % PER_COL
        table[0, place] = total
        table[1, place] = chain
        total = total + ((valid_ref[chain] + (GROUP - 1)) >> 4 << 4)
    table[2, places[0]] = total


def pack(table, places, refs, row, packed):
    sources = [
        (ref, piece, part)
        for ref in refs
        for piece in range(ref.shape[0])
        for part in range(PER_COL)
    ]
    total = table[2, places[0]]
    for (ref, piece, part), place in zip(sources, places):
        packed[pl.ds(pl.multiple_of(table[0, place], GROUP), SLOT), :] = ref[
            piece, row, part * SLOT : (part + 1) * SLOT, :
        ]
    packed[pl.ds(pl.multiple_of(total, GROUP), BLOCK), :] = jnp.zeros(
        (BLOCK, packed.shape[1]), jnp.bfloat16
    )


def project(packed, weight_ref, weight_t_ref, blocks, base, keys, values, peak):
    inner = weight_ref.shape[1] // 4
    heads, depth = values.shape[0], values.shape[1]
    head_size = inner // heads

    def step(block, peak):
        source = pl.ds(pl.multiple_of(block * BLOCK, BLOCK), BLOCK)
        place = pl.ds(pl.multiple_of(base + block * BLOCK, BLOCK), BLOCK)
        part = packed[source, :]
        key_part = jnp.dot(
            part, weight_ref[:, inner : 2 * inner], preferred_element_type=jnp.float32
        )
        turned = lax.dot_general(
            weight_t_ref[2 * inner : 3 * inner, :], part, NT, preferred_element_type=jnp.float32
        ).astype(jnp.bfloat16)
        keys[place, :] = key_part.astype(jnp.bfloat16)
        for h in range(heads):
            values[h, 0:head_size, place] = turned[h * head_size : (h + 1) * head_size]
            values[h, head_size:, place] = jnp.ones((depth - head_size, BLOCK), jnp.bfloat16)
        return jnp.maximum(
            peak, jnp.max(jnp.abs(key_part).reshape(BLOCK // 8, 8, inner), axis=0)
        )

    return lax.fori_loop(0, blocks, step, peak)


def near_kernel(
    valid_ref,
    own_ref,
    sides_ref,
    across_ref,
    left_own_ref,
    left_sides_ref,
    left_across_ref,
    right_own_ref,
    right_sides_ref,
    right_across_ref,
    weight_ref,
    weight_t_ref,
    keys_ref,
    values_ref,
    queries_ref,
    gates_ref,
    peaks_ref,
    packed,
    table,
):
    heads = queries_ref.shape[0]
    inner = queries_ref.shape[2]
    head_size = inner // heads
    own = own_ref[0, 0]
    turned = lax.dot_general(weight_t_ref[0:inner, :], own, NT, preferred_element_type=jnp.float32)
    turned = (turned * head_size ** (-0.5)).astype(jnp.bfloat16)
    gate = jax.nn.sigmoid(
        lax.dot_general(
            weight_t_ref[3 * inner : 4 * inner, :], own, NT, preferred_element_type=jnp.float32
        )
    )
    queries_ref[...] = jnp.zeros_like(queries_ref)
    for h in range(heads):
        span = slice(h * head_size, (h + 1) * head_size)
        queries_ref[h, 0, span, :] = turned[span]
        gates_ref[h, 0] = gate[span]
    places = range(NEAR)

    @pl.when(pl.program_id(0) == 0)
    def _():
        chart(valid_ref, table, places)

    refs = (
        own_ref,
        sides_ref,
        across_ref,
        left_own_ref,
        left_sides_ref,
        left_across_ref,
        right_own_ref,
        right_sides_ref,
        right_across_ref,
    )
    pack(table, places, refs, 0, packed)
    blocks = (table[2, 0] + (BLOCK - 1)) >> 8
    peaks_ref[0] = project(
        packed,
        weight_ref,
        weight_t_ref,
        blocks,
        0,
        keys_ref.at[0],
        values_ref.at[0],
        jnp.zeros((8, inner), jnp.float32),
    )


def piece_spec(piece):
    count, _, cols, width = piece.shape
    return pl.BlockSpec((count, 1, cols, width), lambda i: (0, i, 0, 0))


def fixed(array):
    zeros = (0,) * array.ndim
    return pl.BlockSpec(array.shape, lambda i: zeros, pipeline_mode=pl.Buffered(1))


def project_near(chain_valid, pieces, weight, weight_t, heads):
    _, rows, cols, width = pieces[0].shape
    inner = weight.shape[1] // 4
    head_size = inner // heads
    depth = head_size + GROUP
    return pl.pallas_call(
        near_kernel,
        grid=(rows,),
        in_specs=[
            SMEM,
            *(piece_spec(piece) for piece in pieces),
            fixed(weight),
            fixed(weight_t),
        ],
        out_specs=(
            pl.BlockSpec((1, NEAR_ROOM, inner), lambda i: (i, 0, 0)),
            pl.BlockSpec((1, heads, depth, NEAR_ROOM), lambda i: (i, 0, 0, 0)),
            pl.BlockSpec((heads, 1, inner, cols), lambda i: (0, i, 0, 0)),
            pl.BlockSpec((heads, 1, head_size, cols), lambda i: (0, i, 0, 0)),
            pl.BlockSpec((1, 8, inner), lambda i: (i, 0, 0)),
        ),
        out_shape=(
            jax.ShapeDtypeStruct((rows, NEAR_ROOM, inner), jnp.bfloat16),
            jax.ShapeDtypeStruct((rows, heads, depth, NEAR_ROOM), jnp.bfloat16),
            jax.ShapeDtypeStruct((heads, rows, inner, cols), jnp.bfloat16),
            jax.ShapeDtypeStruct((heads, rows, head_size, cols), jnp.float32),
            jax.ShapeDtypeStruct((rows, 8, inner), jnp.float32),
        ),
        scratch_shapes=[
            pltpu.VMEM((NEAR * SLOT + BLOCK, width), jnp.bfloat16),
            pltpu.SMEM((3, NEAR + FAR), jnp.int32),
        ],
        name="near",
    )(chain_valid, *pieces, weight, weight_t)


def attend_kernel(
    valid_ref,
    keys_hbm,
    values_hbm,
    low_ref,
    high_ref,
    weight_ref,
    weight_t_ref,
    queries,
    peaks_ref,
    gates,
    bias_ref,
    out_weight_ref,
    out_ref,
    keys,
    values,
    packed,
    gated,
    bias,
    shifted,
    sums,
    table,
    safe,
    sems,
):
    heads, rows, inner, cols = queries.shape
    head_size = inner // heads
    head = pl.program_id(0)
    half = bias_ref.shape[0]
    y_low = lax.axis_index("rows") >> 4
    spans = ((0, range(NEAR)), (NEAR_ROOM, range(NEAR, NEAR + FAR)))
    key_copy = pltpu.make_async_copy(keys_hbm, keys.at[:, pl.ds(0, NEAR_ROOM), :], sems.at[heads])

    def value_copy(h):
        return pltpu.make_async_copy(
            values_hbm.at[:, h], values.at[:, h, :, pl.ds(0, NEAR_ROOM)], sems.at[h]
        )

    @pl.when(head == 0)
    def _():
        key_copy.start()
        for h in range(heads):
            value_copy(h).start()
        for _, places in spans:
            chart(valid_ref, table, places)
        far = range(NEAR, NEAR + FAR)
        blocks = (table[2, NEAR] + (BLOCK - 1)) >> 8
        best = jnp.float32(0.0)
        for row in range(rows):
            pack(table, far, (low_ref, high_ref), row, packed)
            peak = project(
                packed,
                weight_ref,
                weight_t_ref,
                blocks,
                NEAR_ROOM,
                keys.at[row],
                values.at[row],
                peaks_ref[row],
            )
            peak = jnp.max(peak, axis=0, keepdims=True)
            peak = jnp.transpose(jnp.broadcast_to(peak, (inner, inner)))[:, 0:1]
            for h in range(heads):
                span = slice(h * head_size, (h + 1) * head_size)
                spread = jnp.abs(queries[h, row, span, :].astype(jnp.float32)) * peak[span]
                best = jnp.maximum(best, jnp.max(jnp.sum(spread, axis=0, keepdims=True)))
        safe[0] = (best < REACH).astype(jnp.int32)
        key_copy.wait()

    for h in range(heads):

        @pl.when(head == h)
        def _(h=h):
            value_copy(h).wait()

    top = jnp.full((GROUP, cols), MASKED, jnp.bfloat16)
    counts = []
    for base, places in spans:
        total = table[2, places[0]]

        def move(place, top, base=base):
            start, chain = table[0, place], table[1, place]
            piece = bias_ref[chain & (half - 1), (chain >> 4) ^ y_low, 0]
            bias[pl.ds(pl.multiple_of(base + start, GROUP), SLOT), :] = piece
            for group in range(0, SLOT, GROUP):
                top = jnp.maximum(top, piece[group : group + GROUP])
            return top

        top = lax.fori_loop(places[0], places[-1] + 1, move, top, unroll=4)
        bias[pl.ds(pl.multiple_of(base + total, GROUP), BLOCK), :] = jnp.full(
            (BLOCK, cols), MASKED, jnp.bfloat16
        )
        counts.append((total + (BLOCK - 1)) >> 8)
    near_blocks, blocks = counts[0], counts[0] + counts[1]
    top = jnp.max(top.astype(jnp.float32), axis=0, keepdims=True)
    sums[...] = jnp.zeros_like(sums)

    def place_of(block):
        block = jnp.where(block < near_blocks, block, block - near_blocks + NEAR_ROOM // BLOCK)
        return pl.ds(pl.multiple_of(block * BLOCK, BLOCK), BLOCK)

    @pl.when(safe[0] == 1)
    def _():
        def span(first, count):
            parts = [place_of(first + n) for n in range(count)]
            for n, place in enumerate(parts):
                shifted[n] = (bias[place, :].astype(jnp.float32) - top) * LOG2E
            weights = []
            for n, place in enumerate(parts):
                scores = [
                    jnp.dot(keys[row, place, :], queries[head, row], preferred_element_type=jnp.float32) for row in range(rows)
                ]
                weights.append(
                    [jnp.exp2(part * LOG2E + shifted[n]).astype(jnp.bfloat16) for part in scores]
                )
            for n, place in enumerate(parts):
                for row in range(rows):
                    sums[row] += jnp.dot(
                        values[row, head, :, place], weights[n][row], preferred_element_type=jnp.float32
                    )

        def double(pair, carry):
            span(2 * pair, 2)
            return carry

        lax.fori_loop(0, blocks >> 1, double, 0)

        @pl.when((blocks & 1) == 1)
        def _():
            span(blocks - 1, 1)

    @pl.when(safe[0] == 0)
    def _():
        def step(block, state):
            place = place_of(block)
            bias_block = bias[place, :].astype(jnp.float32)
            fresh = []
            for row in range(rows):
                scores = jnp.dot(
                    keys[row, place, :], queries[head, row], preferred_element_type=jnp.float32
                )
                scores = scores + bias_block
                new_max = jnp.maximum(state[row], jnp.max(scores, axis=0, keepdims=True))
                weights = jnp.exp(scores - new_max).astype(jnp.bfloat16)
                weighted = jnp.dot(
                    values[row, head, :, place], weights, preferred_element_type=jnp.float32
                )
                sums[row] = sums[row] * jnp.exp(state[row] - new_max) + weighted
                fresh.append(new_max)
            return tuple(fresh)

        lax.fori_loop(
            0,
            blocks,
            step,
            tuple(jnp.full((1, cols), -jnp.inf, jnp.float32) for _ in range(rows)),
        )

    for row in range(rows):
        total_row = sums[row]
        attended = total_row[0:head_size] / total_row[head_size : head_size + 1]
        gated[row, pl.ds(pl.multiple_of(head * head_size, head_size), head_size), :] = (
            attended * gates[0, row]
        ).astype(jnp.bfloat16)

    @pl.when(head == heads - 1)
    def _():
        for row in range(rows):
            out_ref[row] = lax.dot_general(
                gated[row], out_weight_ref[...], TN, preferred_element_type=jnp.float32
            ).astype(jnp.bfloat16)


def attend(
    chain_valid, keys, values, far, weight, weight_t, queries, peaks, gates, bias, output_weight
):
    heads, rows, inner, cols = queries.shape
    depth = values.shape[2]
    half, pair, _, slot, _ = bias.shape
    width = output_weight.shape[1]
    return pl.pallas_call(
        attend_kernel,
        grid=(heads,),
        in_specs=[
            SMEM,
            pl.BlockSpec(memory_space=pl.ANY),
            pl.BlockSpec(memory_space=pl.ANY),
            *(fixed(piece) for piece in far),
            fixed(weight),
            fixed(weight_t),
            fixed(queries),
            fixed(peaks),
            pl.BlockSpec((1, rows, inner // heads, cols), lambda h: (h, 0, 0, 0)),
            pl.BlockSpec((half, pair, 1, slot, cols), lambda h: (0, 0, h, 0, 0)),
            fixed(output_weight),
        ],
        out_specs=pl.BlockSpec((rows, cols, width), lambda h: (0, 0, 0)),
        scratch_shapes=[
            pltpu.VMEM((rows, ROOM, inner), jnp.bfloat16),
            pltpu.VMEM((rows, heads, depth, ROOM), jnp.bfloat16),
            pltpu.VMEM((FAR_ROOM, weight.shape[0]), jnp.bfloat16),
            pltpu.VMEM((rows, inner, cols), jnp.bfloat16),
            pltpu.VMEM((ROOM, cols), jnp.bfloat16),
            pltpu.VMEM((2, BLOCK, cols), jnp.float32),
            pltpu.VMEM((rows, depth, cols), jnp.float32),
            pltpu.SMEM((3, NEAR + FAR), jnp.int32),
            pltpu.SMEM((1,), jnp.int32),
            pltpu.SemaphoreType.DMA((heads + 1,)),
        ],
        out_shape=jax.ShapeDtypeStruct((rows, cols, width), jnp.bfloat16),
        name="attend",
    )(
        chain_valid,
        keys,
        values,
        *far,
        weight,
        weight_t,
        queries,
        peaks,
        gates,
        bias,
        output_weight,
    )


def shift(value, x_step, y_step):
    pairs = [
        (x * YS + y, (x + x_step) % XS * YS + (y + y_step) % YS)
        for x in range(XS)
        for y in range(YS)
    ]
    return lax.ppermute(value, "cols", pairs)


def gather_bias(bias_t):
    count = lax.axis_size("rows")
    half = count // 2
    swapped = lax.ppermute(bias_t, "rows", [(r, (r + half) % count) for r in range(count)])
    both = jnp.stack([bias_t, swapped])
    groups = [list(range(half)), list(range(half, count))]
    return lax.all_gather(both, "rows", axis_index_groups=groups)


def finish(chain_valid, near, far, bias, project_weight, output_weight, heads):
    weight_t = project_weight.T
    keys, values, queries, gates, peaks = project_near(
        chain_valid, near, project_weight, weight_t, heads
    )
    return attend(
        chain_valid,
        keys,
        values,
        far,
        project_weight,
        weight_t,
        queries,
        peaks,
        gates,
        bias,
        output_weight,
    )


def local(pair_rep, project_weight, output_weight, pair_bias, chain_valid):
    normed, bias_t = prep(pair_rep, pair_bias, chain_valid)
    bias = gather_bias(bias_t)
    left_own = shift(normed, 1, 0)
    right_own = shift(normed, -1, 0)
    above = shift(normed, 0, 1)
    below = shift(normed, 0, -1)
    half = normed.shape[0] // 2
    across_low = shift(above[:half], 0, 1)
    across_high = shift(below[half:], 0, -1)
    across = jnp.concatenate([across_low, across_high])
    sides = jnp.stack([above, below])
    left_sides = shift(sides, 1, 0)
    right_sides = shift(sides, -1, 0)
    left_across = shift(across, 1, 0)
    right_across = shift(across, -1, 0)
    far_low = shift(jnp.stack([left_own, left_sides[0]]), 1, 0)
    far_high = shift(jnp.stack([right_sides[1], right_across]), -1, 0)
    near = (
        normed[None],
        sides,
        across[None],
        left_own[None],
        left_sides,
        left_across[None],
        right_own[None],
        right_sides,
        right_across[None],
    )
    return finish(
        chain_valid,
        near,
        (far_low, far_high),
        bias,
        project_weight,
        output_weight,
        pair_bias.shape[0],
    )


def solution(mesh):
    return jax.shard_map(
        local,
        mesh=mesh,
        in_specs=(P("rows", "cols", None), P(), P(), P(None, "cols", "rows"), P()),
        out_specs=P("rows", "cols", None),
        check_vma=False,
    )
```

```python
import jax
import jax.numpy as jnp
from jax import lax
from jax.experimental import pallas as pl
from jax.experimental.pallas import tpu as pltpu
from jax.sharding import PartitionSpec as P


SLOT = 128
GROUP = 16
BLOCK = 256
MASKED = -1000000000.0
LOG2E = 1.4426950408889634
REACH = 60.0
XS, YS = 4, 4
PER_COL = 2
NEAR = 12 * PER_COL
FAR = 4 * PER_COL
NEAR_ROOM = NEAR * SLOT + BLOCK
FAR_ROOM = FAR * SLOT + BLOCK
ROOM = NEAR_ROOM + FAR_ROOM

NT = (((1,), (1,)), ((), ()))
TN = (((0,), (0,)), ((), ()))

SMEM = pl.BlockSpec(memory_space=pltpu.SMEM)
VMEM = pl.BlockSpec(memory_space=pltpu.VMEM)


def prep_kernel(valid_ref, pair_ref, bias_ref, normed_ref, biast_ref):
    pair = pair_ref[...].astype(jnp.float32)
    center = jnp.mean(pair, axis=-1, keepdims=True)
    spread = jnp.mean(jnp.square(pair - center), axis=-1, keepdims=True)
    normed_ref[...] = ((pair - center) * lax.rsqrt(spread + 1e-05)).astype(jnp.bfloat16)
    heads, queries, keys = bias_ref.shape
    valid = valid_ref[lax.axis_index("rows")]
    live = lax.broadcasted_iota(jnp.int32, (keys, queries), 0) < valid
    for head in range(heads):
        turned = jnp.transpose(bias_ref[head].astype(jnp.float32))
        biast_ref[head] = jnp.where(live, turned, MASKED).astype(jnp.bfloat16)


def prep(pair_rep, pair_bias, chain_valid):
    heads, queries, keys = pair_bias.shape
    return pl.pallas_call(
        prep_kernel,
        out_shape=(
            jax.ShapeDtypeStruct(pair_rep.shape, jnp.bfloat16),
            jax.ShapeDtypeStruct((heads, keys, queries), jnp.bfloat16),
        ),
        in_specs=[SMEM, VMEM, VMEM],
        out_specs=(VMEM, VMEM),
        name="prep",
    )(chain_valid, pair_rep, pair_bias)


def chart(valid_ref, table, places):
    col = lax.axis_index("cols")
    x, y = col >> 2, col & 3
    total = jnp.int32(0)
    for place in places:
        x_step = (0, 3, 1, 2)[place // (YS * PER_COL)]
        y_step = (0, 3, 1, 2)[place // PER_COL % YS]
        from_col = ((x + x_step) & (XS - 1)) * YS + ((y + y_step) & (YS - 1))
        chain = from_col * PER_COL + place % PER_COL
        table[0, place] = total
        table[1, place] = chain
        total = total + ((valid_ref[chain] + (GROUP - 1)) >> 4 << 4)
    table[2, places[0]] = total


def pack(table, places, refs, row, packed):
    sources = [
        (ref, piece, part)
        for ref in refs
        for piece in range(ref.shape[0])
        for part in range(PER_COL)
    ]
    total = table[2, places[0]]
    for (ref, piece, part), place in zip(sources, places):
        packed[pl.ds(pl.multiple_of(table[0, place], GROUP), SLOT), :] = ref[
            piece, row, part * SLOT : (part + 1) * SLOT, :
        ]
    packed[pl.ds(pl.multiple_of(total, GROUP), BLOCK), :] = jnp.zeros(
        (BLOCK, packed.shape[1]), jnp.bfloat16
    )


def project(packed, weight_ref, weight_t_ref, blocks, base, keys, values, peak):
    inner = weight_ref.shape[1] // 4
    heads, depth = values.shape[0], values.shape[1]
    head_size = inner // heads

    def step(block, peak):
        source = pl.ds(pl.multiple_of(block * BLOCK, BLOCK), BLOCK)
        place = pl.ds(pl.multiple_of(base + block * BLOCK, BLOCK), BLOCK)
        part = packed[source, :]
        key_part = jnp.dot(
            part, weight_ref[:, inner : 2 * inner], preferred_element_type=jnp.float32
        )
        turned = lax.dot_general(
            weight_t_ref[2 * inner : 3 * inner, :], part, NT, preferred_element_type=jnp.float32
        ).astype(jnp.bfloat16)
        keys[place, :] = key_part.astype(jnp.bfloat16)
        for h in range(heads):
            values[h, 0:head_size, place] = turned[h * head_size : (h + 1) * head_size]
            values[h, head_size:, place] = jnp.ones((depth - head_size, BLOCK), jnp.bfloat16)
        return jnp.maximum(
            peak, jnp.max(jnp.abs(key_part).reshape(BLOCK // 8, 8, inner), axis=0)
        )

    return lax.fori_loop(0, blocks, step, peak)


def near_kernel(
    valid_ref,
    own_ref,
    sides_ref,
    across_ref,
    left_own_ref,
    left_sides_ref,
    left_across_ref,
    right_own_ref,
    right_sides_ref,
    right_across_ref,
    weight_ref,
    weight_t_ref,
    keys_ref,
    values_ref,
    queries_ref,
    gates_ref,
    peaks_ref,
    packed,
    table,
):
    heads = queries_ref.shape[0]
    inner = queries_ref.shape[2]
    head_size = inner // heads
    own = own_ref[0, 0]
    turned = lax.dot_general(weight_t_ref[0:inner, :], own, NT, preferred_element_type=jnp.float32)
    turned = (turned * head_size ** (-0.5)).astype(jnp.bfloat16)
    gate = jax.nn.sigmoid(
        lax.dot_general(
            weight_t_ref[3 * inner : 4 * inner, :], own, NT, preferred_element_type=jnp.float32
        )
    )
    queries_ref[...] = jnp.zeros_like(queries_ref)
    for h in range(heads):
        span = slice(h * head_size, (h + 1) * head_size)
        queries_ref[h, 0, span, :] = turned[span]
        gates_ref[h, 0] = gate[span]
    places = range(NEAR)

    @pl.when(pl.program_id(0) == 0)
    def _():
        chart(valid_ref, table, places)

    refs = (
        own_ref,
        sides_ref,
        across_ref,
        left_own_ref,
        left_sides_ref,
        left_across_ref,
        right_own_ref,
        right_sides_ref,
        right_across_ref,
    )
    pack(table, places, refs, 0, packed)
    blocks = (table[2, 0] + (BLOCK - 1)) >> 8
    peaks_ref[0] = project(
        packed,
        weight_ref,
        weight_t_ref,
        blocks,
        0,
        keys_ref.at[0],
        values_ref.at[0],
        jnp.zeros((8, inner), jnp.float32),
    )


def piece_spec(piece):
    count, _, cols, width = piece.shape
    return pl.BlockSpec((count, 1, cols, width), lambda i: (0, i, 0, 0))


def fixed(array):
    zeros = (0,) * array.ndim
    return pl.BlockSpec(array.shape, lambda i: zeros, pipeline_mode=pl.Buffered(1))


def project_near(chain_valid, pieces, weight, weight_t, heads):
    _, rows, cols, width = pieces[0].shape
    inner = weight.shape[1] // 4
    head_size = inner // heads
    depth = head_size + GROUP
    return pl.pallas_call(
        near_kernel,
        grid=(rows,),
        in_specs=[
            SMEM,
            *(piece_spec(piece) for piece in pieces),
            fixed(weight),
            fixed(weight_t),
        ],
        out_specs=(
            pl.BlockSpec((1, NEAR_ROOM, inner), lambda i: (i, 0, 0)),
            pl.BlockSpec((1, heads, depth, NEAR_ROOM), lambda i: (i, 0, 0, 0)),
            pl.BlockSpec((heads, 1, inner, cols), lambda i: (0, i, 0, 0)),
            pl.BlockSpec((heads, 1, head_size, cols), lambda i: (0, i, 0, 0)),
            pl.BlockSpec((1, 8, inner), lambda i: (i, 0, 0)),
        ),
        out_shape=(
            jax.ShapeDtypeStruct((rows, NEAR_ROOM, inner), jnp.bfloat16),
            jax.ShapeDtypeStruct((rows, heads, depth, NEAR_ROOM), jnp.bfloat16),
            jax.ShapeDtypeStruct((heads, rows, inner, cols), jnp.bfloat16),
            jax.ShapeDtypeStruct((heads, rows, head_size, cols), jnp.float32),
            jax.ShapeDtypeStruct((rows, 8, inner), jnp.float32),
        ),
        scratch_shapes=[
            pltpu.VMEM((NEAR * SLOT + BLOCK, width), jnp.bfloat16),
            pltpu.SMEM((3, NEAR + FAR), jnp.int32),
        ],
        name="near",
    )(chain_valid, *pieces, weight, weight_t)


def attend_kernel(
    valid_ref,
    keys_hbm,
    values_hbm,
    low_ref,
    high_ref,
    weight_ref,
    weight_t_ref,
    queries,
    peaks_ref,
    gates,
    bias_ref,
    out_weight_ref,
    out_ref,
    keys,
    values,
    packed,
    gated,
    bias,
    shifted,
    sums,
    table,
    safe,
    sems,
):
    heads, rows, inner, cols = queries.shape
    head_size = inner // heads
    head = pl.program_id(0)
    half = bias_ref.shape[0]
    y_low = lax.axis_index("rows") >> 4
    spans = ((0, range(NEAR)), (NEAR_ROOM, range(NEAR, NEAR + FAR)))
    key_copy = pltpu.make_async_copy(keys_hbm, keys.at[:, pl.ds(0, NEAR_ROOM), :], sems.at[heads])

    def value_copy(h):
        return pltpu.make_async_copy(
            values_hbm.at[:, h], values.at[:, h, :, pl.ds(0, NEAR_ROOM)], sems.at[h]
        )

    @pl.when(head == 0)
    def _():
        key_copy.start()
        for h in range(heads):
            value_copy(h).start()
        for _, places in spans:
            chart(valid_ref, table, places)
        far = range(NEAR, NEAR + FAR)
        blocks = (table[2, NEAR] + (BLOCK - 1)) >> 8
        best = jnp.float32(0.0)
        for row in range(rows):
            pack(table, far, (low_ref, high_ref), row, packed)
            peak = project(
                packed,
                weight_ref,
                weight_t_ref,
                blocks,
                NEAR_ROOM,
                keys.at[row],
                values.at[row],
                peaks_ref[row],
            )
            peak = jnp.max(peak, axis=0, keepdims=True)
            peak = jnp.transpose(jnp.broadcast_to(peak, (inner, inner)))[:, 0:1]
            for h in range(heads):
                span = slice(h * head_size, (h + 1) * head_size)
                spread = jnp.abs(queries[h, row, span, :].astype(jnp.float32)) * peak[span]
                best = jnp.maximum(best, jnp.max(jnp.sum(spread, axis=0, keepdims=True)))
        safe[0] = (best < REACH).astype(jnp.int32)
        key_copy.wait()

    for h in range(heads):

        @pl.when(head == h)
        def _(h=h):
            value_copy(h).wait()

    top = jnp.full((GROUP, cols), MASKED, jnp.bfloat16)
    counts = []
    for base, places in spans:
        total = table[2, places[0]]

        def move(place, top, base=base):
            start, chain = table[0, place], table[1, place]
            piece = bias_ref[chain & (half - 1), (chain >> 4) ^ y_low, 0]
            bias[pl.ds(pl.multiple_of(base + start, GROUP), SLOT), :] = piece
            for group in range(0, SLOT, GROUP):
                top = jnp.maximum(top, piece[group : group + GROUP])
            return top

        top = lax.fori_loop(places[0], places[-1] + 1, move, top, unroll=4)
        bias[pl.ds(pl.multiple_of(base + total, GROUP), BLOCK), :] = jnp.full(
            (BLOCK, cols), MASKED, jnp.bfloat16
        )
        counts.append((total + (BLOCK - 1)) >> 8)
    near_blocks, blocks = counts[0], counts[0] + counts[1]
    top = jnp.max(top.astype(jnp.float32), axis=0, keepdims=True)
    sums[...] = jnp.zeros_like(sums)

    def place_of(block):
        block = jnp.where(block < near_blocks, block, block - near_blocks + NEAR_ROOM // BLOCK)
        return pl.ds(pl.multiple_of(block * BLOCK, BLOCK), BLOCK)

    @pl.when(safe[0] == 1)
    def _():
        def span(first, count):
            parts = [place_of(first + n) for n in range(count)]
            for n, place in enumerate(parts):
                shifted[n] = (bias[place, :].astype(jnp.float32) - top) * LOG2E

            def score(place):
                return [
                    jnp.dot(
                        keys[row, place, :], queries[head, row], preferred_element_type=jnp.float32
                    )
                    for row in range(rows)
                ]

            def weigh(n, scores):
                return [
                    jnp.exp2(part * LOG2E + shifted[n]).astype(jnp.bfloat16) for part in scores
                ]

            weights = [weigh(n, score(place)) for n, place in enumerate(parts)]
            for row in range(rows):
                fresh = sums[row]
                for n, place in enumerate(parts):
                    fresh += jnp.dot(
                        values[row, head, :, place], weights[n][row], preferred_element_type=jnp.float32
                    )
                sums[row] = fresh

        def double(pair, carry):
            span(2 * pair, 2)
            return carry

        lax.fori_loop(0, blocks >> 1, double, 0)

        @pl.when((blocks & 1) == 1)
        def _():
            span(blocks - 1, 1)

    @pl.when(safe[0] == 0)
    def _():
        def step(block, state):
            place = place_of(block)
            bias_block = bias[place, :].astype(jnp.float32)
            fresh = []
            for row in range(rows):
                scores = jnp.dot(
                    keys[row, place, :], queries[head, row], preferred_element_type=jnp.float32
                )
                scores = scores + bias_block
                new_max = jnp.maximum(state[row], jnp.max(scores, axis=0, keepdims=True))
                weights = jnp.exp(scores - new_max).astype(jnp.bfloat16)
                weighted = jnp.dot(
                    values[row, head, :, place], weights, preferred_element_type=jnp.float32
                )
                sums[row] = sums[row] * jnp.exp(state[row] - new_max) + weighted
                fresh.append(new_max)
            return tuple(fresh)

        lax.fori_loop(
            0,
            blocks,
            step,
            tuple(jnp.full((1, cols), -jnp.inf, jnp.float32) for _ in range(rows)),
        )

    for row in range(rows):
        total_row = sums[row]
        attended = total_row[0:head_size] / total_row[head_size : head_size + 1]
        gated[row, pl.ds(pl.multiple_of(head * head_size, head_size), head_size), :] = (
            attended * gates[0, row]
        ).astype(jnp.bfloat16)

    @pl.when(head == heads - 1)
    def _():
        for row in range(rows):
            out_ref[row] = lax.dot_general(
                gated[row], out_weight_ref[...], TN, preferred_element_type=jnp.float32
            ).astype(jnp.bfloat16)


def attend(
    chain_valid, keys, values, far, weight, weight_t, queries, peaks, gates, bias, output_weight
):
    heads, rows, inner, cols = queries.shape
    depth = values.shape[2]
    half, pair, _, slot, _ = bias.shape
    width = output_weight.shape[1]
    return pl.pallas_call(
        attend_kernel,
        grid=(heads,),
        in_specs=[
            SMEM,
            pl.BlockSpec(memory_space=pl.ANY),
            pl.BlockSpec(memory_space=pl.ANY),
            *[VMEM] * len(far),
            fixed(weight),
            fixed(weight_t),
            fixed(queries),
            fixed(peaks),
            pl.BlockSpec((1, rows, inner // heads, cols), lambda h: (h, 0, 0, 0)),
            pl.BlockSpec((half, pair, 1, slot, cols), lambda h: (0, 0, h, 0, 0)),
            fixed(output_weight),
        ],
        out_specs=pl.BlockSpec((rows, cols, width), lambda h: (0, 0, 0)),
        scratch_shapes=[
            pltpu.VMEM((rows, ROOM, inner), jnp.bfloat16),
            pltpu.VMEM((rows, heads, depth, ROOM), jnp.bfloat16),
            pltpu.VMEM((FAR_ROOM, weight.shape[0]), jnp.bfloat16),
            pltpu.VMEM((rows, inner, cols), jnp.bfloat16),
            pltpu.VMEM((ROOM, cols), jnp.bfloat16),
            pltpu.VMEM((2, BLOCK, cols), jnp.float32),
            pltpu.VMEM((rows, depth, cols), jnp.float32),
            pltpu.SMEM((3, NEAR + FAR), jnp.int32),
            pltpu.SMEM((1,), jnp.int32),
            pltpu.SemaphoreType.DMA((heads + 1,)),
        ],
        out_shape=jax.ShapeDtypeStruct((rows, cols, width), jnp.bfloat16),
        name="attend",
    )(
        chain_valid,
        keys,
        values,
        *far,
        weight,
        weight_t,
        queries,
        peaks,
        gates,
        bias,
        output_weight,
    )


def shift(value, x_step, y_step):
    pairs = [
        (x * YS + y, (x + x_step) % XS * YS + (y + y_step) % YS)
        for x in range(XS)
        for y in range(YS)
    ]
    return lax.ppermute(value, "cols", pairs)


def gather_bias(bias_t):
    count = lax.axis_size("rows")
    half = count // 2
    swapped = lax.ppermute(bias_t, "rows", [(r, (r + half) % count) for r in range(count)])
    both = jnp.stack([bias_t, swapped])
    groups = [list(range(half)), list(range(half, count))]
    return lax.all_gather(both, "rows", axis_index_groups=groups)


def finish(chain_valid, near, far, bias, project_weight, output_weight, heads):
    weight_t = project_weight.T
    keys, values, queries, gates, peaks = project_near(
        chain_valid, near, project_weight, weight_t, heads
    )
    return attend(
        chain_valid,
        keys,
        values,
        far,
        project_weight,
        weight_t,
        queries,
        peaks,
        gates,
        bias,
        output_weight,
    )


def local(pair_rep, project_weight, output_weight, pair_bias, chain_valid):
    normed, bias_t = prep(pair_rep, pair_bias, chain_valid)
    bias = gather_bias(bias_t)
    left_own = shift(normed, 1, 0)
    right_own = shift(normed, -1, 0)
    above = shift(normed, 0, 1)
    below = shift(normed, 0, -1)
    half = normed.shape[0] // 2
    across_low = shift(above[:half], 0, 1)
    across_high = shift(below[half:], 0, -1)
    across = jnp.concatenate([across_low, across_high])
    sides = jnp.stack([above, below])
    left_sides = shift(sides, 1, 0)
    right_sides = shift(sides, -1, 0)
    left_across = shift(across, 1, 0)
    right_across = shift(across, -1, 0)
    far_low = shift(jnp.stack([left_own, left_sides[0]]), 1, 0)
    far_high = shift(jnp.stack([right_sides[1], right_across]), -1, 0)
    near = (
        normed[None],
        sides,
        across[None],
        left_own[None],
        left_sides,
        left_across[None],
        right_own[None],
        right_sides,
        right_across[None],
    )
    return finish(
        chain_valid,
        near,
        (far_low, far_high),
        bias,
        project_weight,
        output_weight,
        pair_bias.shape[0],
    )


def solution(mesh):
    return jax.shard_map(
        local,
        mesh=mesh,
        in_specs=(P("rows", "cols", None), P(), P(), P(None, "cols", "rows"), P()),
        out_specs=P("rows", "cols", None),
        check_vma=False,
    )
```
